128 devices in a mesh: blk: 32 (over z, x, core), nb: 4 (over y).
Axes of the slice: x: 4, y: 4, z: 4, core: 2. Of those that a mesh axis runs over, the one named last changes fastest.
Arguments:
- latent: float32 [1024, 96, 128], P(('blk', 'nb')), may hold values from -8 to 8
- coords: float32 [1024, 2, 128], P(('blk', 'nb')), may hold values from 0 to 1
- labels: int32 [1024, 96, 128], P(('blk', 'nb')), may hold values 0 or 1
- owner: int32 [1024, 4], P(('blk', 'nb')), may hold values from 0 to 127, all different within a row; in each aligned block of 8 rows (0 to 7, 8 to 15, ...) at most 2 rows name the same one
- slot: int32 [1024, 4], P(('blk', 'nb')), may hold values from 0 to 7
Outputs:
- new_latent: float32 [1024, 96, 128], P(('blk', 'nb'))
- step_rms: float32 [96], replicated
The draws below stay inside these ranges and needn't reach their ends.
Inputs may be any that keep to these rules, and one draw needn't show every extreme that they name: The 4 owners of one block are distinct; the 8 blocks stored on one device name any one owner at most 2 times.
All inputs are finite; a program needn't handle non-finite values. No bound on the sum of `labels` on one device may be relied on, other than what follows from the above.
Results may differ from the reference program's by a relative error of at most 0.0003.
Values sent between devices are 32-bit elements; how exact they have to be, the bound alone decides.
A program may use at most 192 MiB of HBM per device.

```python
import math
import jax
import jax.numpy as jnp
import numpy as np
from jax import lax

PTS = 128
NBR = 4
BLK_DEV = 8
FIELDS = 96
BLOCKS = 1024
CAP = 2
DEVICES = 128


def draw_latent(key, part):
    levels = jnp.exp(jnp.linspace(math.log(0.6), math.log(2.0), BLOCKS, dtype=jnp.float32))
    base = jnp.clip(jax.random.normal(key, (BLOCKS, FIELDS, PTS), jnp.float32), -4.0, 4.0)
    return (base * levels[:, None, None]).astype(jnp.float32)


def plant(values, rng, least, high):
    index_at = [jax.random.randint(jax.random.fold_in(rng, axis), (), 0, length) for axis, length in enumerate(values.shape)]
    longest = values.shape.index(max(values.shape))
    beside = index_at[:longest] + [(index_at[longest] + 1) % values.shape[longest]] + index_at[longest + 1:]
    return values.at[tuple(index_at)].set(least).at[tuple(beside)].set(high)


def block_levels(key, extent, shards, smallest, largest):
    def one(position, blocks):
        heights = jax.random.uniform(jax.random.fold_in(jax.random.fold_in(key, 6), position), (blocks,), jnp.float32, smallest / len(shards), largest / len(shards))
        return jnp.repeat(jnp.exp(heights), extent[position] // blocks).reshape((-1,) + (1,) * (len(extent) - position - 1))

    loudness = one(*shards[0])
    for cut in shards[1:]:
        loudness = loudness * one(*cut)
    return loudness


def deal_out(rng, own, number, rows, number_of, top, bound, lean):
    order = jax.random.permutation(rng, number_of)
    packed, common = load_shares(number_of, rows * top, bound, lean, True), load_shares(number_of, rows * top, bound, lean, False)
    places = jnp.arange(number_of)

    def named(lengths, offset_by):
        used = int((lengths > 0).sum())
        fixed = max(1, used // 4)
        passed = fixed + (places - fixed + offset_by * (used - fixed)) % max(1, number_of - fixed)
        return jnp.zeros((number_of,), jnp.int32).at[order[jnp.where(places < fixed, places, passed)]].set(jnp.asarray(lengths, jnp.int32))

    lengths = jnp.where(number % 4 == 0, named(packed, number // 4), named(common, number - number // 4 - 1))
    mixed = jax.random.permutation(jax.random.fold_in(own, 3), number_of)
    giver, sink = mixed[0:number_of // 2 * 2:2], mixed[1:number_of // 2 * 2:2]
    room = jnp.minimum(lengths[giver] - 1, bound - lengths[sink]) // 2
    room = jnp.where((giver == order[0]) | (sink == order[0]) | (lengths[sink] == 0), 0, jnp.maximum(room, 0))
    passed = jax.random.randint(jax.random.fold_in(own, 4), (number_of // 2,), 0, 1 << 20) % (room + 1)
    lengths = lengths.at[giver].add(-passed).at[sink].add(passed)
    members = jnp.searchsorted(jnp.cumsum(lengths), jnp.arange(rows * top), side="right").astype(jnp.int32)
    listing = members.reshape(top, rows).T
    listing = listing[jax.random.permutation(jax.random.fold_in(own, 1), rows)]
    offset_by = jax.random.randint(jax.random.fold_in(own, 2), (rows, 1), 0, top)
    return jnp.take_along_axis(listing, (jnp.arange(top)[None, :] + offset_by) % top, axis=1)


def load_shares(number_of, total, bound, slope, full):
    weights = [(1 << 20) // math.isqrt(grade ** slope) + 1 for grade in range(1, number_of + 1)]
    largest = bound if full else min(bound, max(-(-total // number_of), total * weights[0] // sum(weights)))
    least = 1 if total - largest >= number_of - 1 else 0
    counts, rest = [largest] + [least] * (number_of - 1), total - largest - least * (number_of - 1)
    while rest > 0:
        movable = [i for i in range(1, number_of) if counts[i] < largest] or [i for i in range(1, number_of) if counts[i] < bound]
        whole, remaining = sum([weights[i] for i in movable]), rest
        for i in movable:
            extra = min(bound - counts[i], max(1, remaining * weights[i] // whole), rest)
            counts[i] = counts[i] + extra
            rest = rest - extra
    return np.array(counts)


def setup_inputs(seed: int = 0) -> dict:
    key_of = jax.random.split(jax.random.key(seed), 6)
    latent = draw_latent(jax.random.fold_in(key_of[5], 71), 0)
    coords = jnp.clip(1.0 * jax.random.uniform(key_of[1], (BLOCKS, 2, PTS), jnp.float32) ** block_levels(key_of[1], (BLOCKS, 2, PTS), ((0, 128),), -0.2, 0.2), 0.0, 1.0)
    labels = plant((jax.random.randint(key_of[2], (BLOCKS, FIELDS, PTS), 0, 2) < 1).astype(jnp.int32), jax.random.fold_in(key_of[2], 1), 0, 1)
    owner_keys = jax.random.split(jax.random.fold_in(key_of[3], 1), BLOCKS // BLK_DEV)
    owner_turns = jax.random.permutation(jax.random.fold_in(key_of[3], 3), BLOCKS // BLK_DEV)
    owner = jax.vmap(lambda own, number: deal_out(jax.random.fold_in(key_of[3], 2), own, number, BLK_DEV, DEVICES, NBR, CAP, 2))(owner_keys, owner_turns).reshape((BLOCKS, NBR))
    slot = plant(jax.random.randint(key_of[4], (BLOCKS, NBR), 0, BLK_DEV), jax.random.fold_in(key_of[4], 1), 0, BLK_DEV - 1).astype(jnp.int32)
    return dict(latent=latent, coords=coords, labels=labels, owner=owner, slot=slot)


nugget = 0.25
length_scale = 0.1

def covariance(points):
    east_gap = points[:, 0, :, None] - points[:, 0, None, :]
    north_gap = points[:, 1, :, None] - points[:, 1, None, :]
    scaled = jnp.sqrt(east_gap * east_gap + north_gap * north_gap) * (math.sqrt(3.0) / length_scale)
    kernel = (1.0 + scaled) * jnp.exp(-scaled)
    matrix_order = points.shape[-1]
    return kernel + nugget * jnp.eye(matrix_order, dtype=jnp.float32)

def factor_group(points, values):
    factor = jnp.linalg.cholesky(covariance(points))
    width = values.shape[-1]
    own_width = width // 5
    split = width - own_width
    whitened = lax.linalg.triangular_solve(factor, values, left_side=False, lower=True, transpose_a=True)
    target = jnp.concatenate([jnp.zeros_like(whitened[..., :split]), whitened[..., split:]], axis=-1)
    pulled = lax.linalg.triangular_solve(factor, target, left_side=False, lower=True, transpose_a=False)
    corner = factor[:, split:, split:]
    identity = jnp.broadcast_to(jnp.eye(own_width, dtype=jnp.float32), corner.shape)
    inverse = lax.linalg.triangular_solve(corner, identity, left_side=True, lower=True)
    return (pulled, lax.optimization_barrier(jnp.sum(inverse * inverse, axis=-2)))

def probit_ratio(margin):
    density = jnp.exp(-0.5 * margin * margin - 0.5 * math.log(2.0 * math.pi))
    mass = 0.5 * lax.erfc(-margin / math.sqrt(2.0))
    return density / mass

def reference(latent, coords, labels, owner, slot):
    blocks = latent.shape[0]
    neighbour = (owner * BLK_DEV + slot).astype(jnp.int32)
    group = math.gcd(blocks, 64)

    def visit(carry, index):
        start = (index * group).astype(jnp.int32)
        near = lax.dynamic_slice_in_dim(neighbour, start, group, 0)
        own_values = lax.dynamic_slice_in_dim(latent, start, group, 0)
        own_points = lax.dynamic_slice_in_dim(coords, start, group, 0)
        near_values = latent[near].transpose(0, 2, 1, 3).reshape(group, FIELDS, NBR * PTS)
        near_points = coords[near].transpose(0, 2, 1, 3).reshape(group, 2, NBR * PTS)
        values = jnp.concatenate([near_values, own_values], axis=-1)
        points = jnp.concatenate([near_points, own_points], axis=-1)
        pulled, precision_diag = factor_group(points, values)
        parts = pulled[..., :NBR * PTS].reshape(group, FIELDS, NBR, PTS).transpose(0, 2, 1, 3)
        carry = carry.at[near.reshape(-1)].add(parts.reshape(group * NBR, FIELDS, PTS))
        return (carry, (pulled[..., NBR * PTS:], precision_diag))
    start_sum = jnp.zeros((blocks, FIELDS, PTS), jnp.float32)
    steps_count = blocks // group
    scattered, outputs = lax.scan(visit, start_sum, jnp.arange(steps_count, dtype=jnp.int32))
    own_grad = outputs[0].reshape(blocks, FIELDS, PTS)
    qdiag = outputs[1].reshape(blocks, PTS)
    prior = scattered + own_grad
    sign = 2.0 * labels.astype(jnp.float32) - 1.0
    margin = sign * latent
    ratio = probit_ratio(margin)
    weight = ratio * (ratio + margin)
    delta = (sign * ratio - prior) / (weight + qdiag[:, None, :])
    spread = lax.optimization_barrier(jnp.sum(delta * delta, axis=(0, 2)))
    step_rms = jnp.sqrt(spread / (blocks * PTS) + 1e-06)
    new_latent = latent + 0.5 * delta / step_rms[None, :, None]
    return (new_latent, step_rms)
```

```python
import math
import functools
import jax
import jax.numpy as jnp
from jax import lax
from jax.experimental import pallas as pl
from jax.experimental.pallas import tpu as pltpu
from jax.sharding import PartitionSpec as P

nugget = 0.25
length_scale = 0.1
HI = lax.Precision.HIGHEST
NN = (((1,), (0,)), ((), ()))
NT = (((1,), (1,)), ((), ()))
TN = (((0,), (0,)), ((), ()))


def dot(a, b, dims=NN):
    return lax.dot_general(a, b, dims, precision=HI, preferred_element_type=jnp.float32)


def sweep64(pack):
    lane = lax.broadcasted_iota(jnp.int32, (64, 128), 1)
    base = lane & 64
    inner = lane & 63

    def step(t, carry):
        p = 2 * t
        at0 = base + p
        at1 = at0 + 1
        own = (inner == p) | (inner == p + 1)
        for q in range(4):
            rows = pack[q, pl.ds(p, 2), :]
            r1 = jnp.broadcast_to(rows[0:1], (8, 128))
            r2 = jnp.broadcast_to(rows[1:2], (8, 128))
            a = jnp.take_along_axis(r1, at0[:8], axis=1)
            b = jnp.take_along_axis(r1, at1[:8], axis=1)
            d = jnp.take_along_axis(r2, at1[:8], axis=1)
            rdet = 1.0 / (a * d - b * b)
            first = inner[:8] == p
            second = inner[:8] == p + 1
            r1 = jnp.where(first, 1.0, jnp.where(second, 0.0, r1))
            r2 = jnp.where(first, 0.0, jnp.where(second, 1.0, r2))
            new1 = (d * r1 - b * r2) * rdet
            new2 = (a * r2 - b * r1) * rdet
            for s in range(8):
                x = pack[q, pl.ds(8 * s, 8), :]
                c1 = jnp.take_along_axis(x, at0[:8], axis=1)
                c2 = jnp.take_along_axis(x, at1[:8], axis=1)
                x = jnp.where(own[:8], 0.0, x)
                pack[q, pl.ds(8 * s, 8), :] = x - c1 * new1 - c2 * new2
            pack[q, pl.ds(p, 2), :] = jnp.concatenate([new1[0:1], new2[0:1]], axis=0)
        return carry

    lax.fori_loop(0, 32, step, 0)


def factor_kernel(nbr_ref, self_ref, coords_ref, own_ref, gt_ref, si_ref, cov, upper, tile, dinv, pack):
    n = own_ref.shape[0]
    near = nbr_ref.shape[1]
    nt = near + 1
    scale = math.sqrt(3.0) / length_scale

    def build(m, carry):
        pts = [coords_ref[nbr_ref[m, k]] for k in range(near)] + [own_ref[m]]
        for i in range(nt):
            xc = jnp.broadcast_to(pts[i][0:1], (128, 128)).T
            yc = jnp.broadcast_to(pts[i][1:2], (128, 128)).T
            for j in range(i + 1):
                dx = xc - pts[j][0:1]
                dy = yc - pts[j][1:2]
                s = jnp.sqrt(dx * dx + dy * dy) * scale
                c = (1.0 + s) * jnp.exp(-s)
                if i == j:
                    r = lax.broadcasted_iota(jnp.int32, (128, 128), 0)
                    q = lax.broadcasted_iota(jnp.int32, (128, 128), 1)
                    c = c + jnp.where(r == q, nugget, 0.0)
                cov[m, i * 128:(i + 1) * 128, j * 128:(j + 1) * 128] = c
        return carry

    lax.fori_loop(0, n, build, 0)

    for j in range(nt):
        lo, hi = j * 128, (j + 1) * 128

        def left(m, carry):
            p = cov[m, lo:, lo:hi]
            if j:
                p = p - dot(upper[m, lo:, :lo], tile[m, lo:hi, :lo], NT)
            tile[m, lo:, lo:hi] = p
            return carry

        lax.fori_loop(0, n, left, 0)

        for q in range(n // 2):
            pack[q] = jnp.concatenate(
                [tile[2 * q, lo:lo + 64, lo:lo + 64], tile[2 * q + 1, lo:lo + 64, lo:lo + 64]], axis=1
            )
        sweep64(pack)
        for m in range(n):
            at = (m % 2) * 64
            ai = pack[m // 2, :, at:at + 64]
            b = tile[m, lo + 64:hi, lo:lo + 64]
            v = dot(b, ai)
            dinv[m, 0:64, 0:64] = ai
            dinv[m, 64:128, 0:64] = v
            dinv[m, 64:128, 64:128] = tile[m, lo + 64:hi, lo + 64:hi] - dot(v, b, NT)
        for q in range(n // 2):
            pack[q] = jnp.concatenate(
                [dinv[2 * q, 64:128, 64:128], dinv[2 * q + 1, 64:128, 64:128]], axis=1
            )
        sweep64(pack)
        for m in range(n):
            at = (m % 2) * 64
            si = pack[m // 2, :, at:at + 64]
            v = dinv[m, 64:128, 0:64]
            w = dot(si, v)
            dinv[m, 64:128, 64:128] = si
            dinv[m, 64:128, 0:64] = -w
            dinv[m, 0:64, 64:128] = -w.T
            dinv[m, 0:64, 0:64] = dinv[m, 0:64, 0:64] + dot(v, w, TN)

        if j < nt - 1:
            def scale_panel(m, carry):
                upper[m, hi:, lo:hi] = dot(tile[m, hi:, lo:hi], dinv[m])
                return carry

            lax.fori_loop(0, n, scale_panel, 0)

    def back(m, carry):
        last = near * 128
        si_ref[m] = dinv[m]
        for k in reversed(range(near)):
            g = upper[m, last:, k * 128:(k + 1) * 128]
            if k < near - 1:
                g = g - dot(gt_ref[m, :, (k + 1) * 128:last], upper[m, (k + 1) * 128:last, k * 128:(k + 1) * 128])
            gt_ref[m, :, k * 128:(k + 1) * 128] = g
        return carry

    lax.fori_loop(0, n, back, 0)


def factor(nbr, coords_all, coords_own):
    n, near = nbr.shape
    width = (near + 1) * 128
    return pl.pallas_call(
        factor_kernel,
        out_shape=(
            jax.ShapeDtypeStruct((n, 128, near * 128), jnp.float32),
            jax.ShapeDtypeStruct((n, 128, 128), jnp.float32),
        ),
        in_specs=[pl.BlockSpec(memory_space=pltpu.SMEM), pl.BlockSpec(memory_space=pltpu.SMEM)]
        + [pl.BlockSpec(memory_space=pltpu.VMEM)] * 2,
        out_specs=(pl.BlockSpec(memory_space=pltpu.VMEM),) * 2,
        scratch_shapes=[
            pltpu.VMEM((n, width, width), jnp.float32),
            pltpu.VMEM((n, width, width - 128), jnp.float32),
            pltpu.VMEM((n, width, width), jnp.float32),
            pltpu.VMEM((n, 128, 128), jnp.float32),
            pltpu.VMEM((n // 2, 64, 128), jnp.float32),
        ],
        compiler_params=pltpu.CompilerParams(vmem_limit_bytes=56 * 1024 * 1024),
        cost_estimate=pl.CostEstimate(flops=2_000_000_000, bytes_accessed=5_000_000, transcendentals=4_000_000),
        name="factor",
    )(nbr, nbr, coords_all, coords_own)


def apply_kernel(nbr_ref, pos_ref, v0_ref, v1_ref, v2_ref, v3_ref, own_ref, gt_ref, si_ref, zero_ref, out_ref, u_ref, keep):
    k = pl.program_id(1)

    @pl.when(k == 0)
    def _():
        r = own_ref[0]
        for i, v in enumerate((v0_ref, v1_ref, v2_ref, v3_ref)):
            r = r - dot(v[0], gt_ref[0, :, i * 128:(i + 1) * 128], NT)
        u = dot(r, si_ref[0])
        keep[...] = u
        u_ref[0] = u

    g = gt_ref[0, :, pl.ds(pl.multiple_of(k * 128, 128), 128)]
    out_ref[0] = -dot(keep[...], g)


def apply_blocks(nbr, pos, latent_all, latent, gt, si, zero):
    n, near = nbr.shape
    fields = latent.shape[1]
    def v_spec(i):
        return pl.BlockSpec((1, fields, 128), lambda b, k, nbr, pos: (nbr[b * near + i], 0, 0))
    def b_spec(*shape):
        return pl.BlockSpec((1,) + shape, lambda b, k, nbr, pos: (b, 0, 0))
    return pl.pallas_call(
        apply_kernel,
        out_shape=(
            jax.ShapeDtypeStruct(zero.shape, jnp.float32),
            jax.ShapeDtypeStruct(latent.shape, jnp.float32),
        ),
        grid_spec=pltpu.PrefetchScalarGridSpec(
            num_scalar_prefetch=2,
            grid=(n, near),
            in_specs=[v_spec(i) for i in range(near)]
            + [b_spec(fields, 128), b_spec(128, near * 128), b_spec(128, 128), pl.BlockSpec(memory_space=pl.ANY)],
            out_specs=(
                pl.BlockSpec((1, fields, 128), lambda b, k, nbr, pos: (pos[b * near + k], 0, 0)),
                b_spec(fields, 128),
            ),
            scratch_shapes=[pltpu.VMEM((fields, 128), jnp.float32)],
        ),
        input_output_aliases={9: 0},
        name="apply",
    )(nbr.reshape(-1), pos.reshape(-1), *([latent_all] * near), latent, gt, si, zero)


def probit_ratio(margin):
    density = jnp.exp(-0.5 * margin * margin - 0.5 * math.log(2.0 * math.pi))
    mass = 0.5 * lax.erfc(-margin / math.sqrt(2.0))
    return density / mass


def body(latent, coords, labels, owner, slot):
    block_count, field_count, point_count = latent.shape
    near_count = owner.shape[1]
    axes = ("blk", "nb")
    device_count = lax.axis_size("blk") * lax.axis_size("nb")
    capacity = max(2, 2 * block_count * near_count // device_count)
    nbr = owner * block_count + slot
    coords_all = lax.all_gather(coords, axes, axis=0, tiled=True)
    latent_all = lax.all_gather(latent, axes, axis=0, tiled=True)
    wanted = owner.reshape(-1)
    places = slot.reshape(-1)
    request_count = wanted.shape[0]
    earlier = lax.broadcasted_iota(
        jnp.int32, (request_count, request_count), 1
    ) < lax.broadcasted_iota(jnp.int32, (request_count, request_count), 0)
    slot_rank = jnp.sum(
        jnp.where((wanted[None, :] == wanted[:, None]) & earlier, 1, 0), axis=1
    ).astype(jnp.int32)
    position = wanted * capacity + slot_rank
    requests = jnp.full((device_count * capacity,), -1, jnp.int32).at[position].set(places)
    kept = lax.all_to_all(
        requests.reshape(device_count, capacity), axes, split_axis=0, concat_axis=0, tiled=True
    )
    gt, si = factor(nbr, coords_all, coords)
    zero = jnp.zeros((device_count * capacity, field_count, point_count), jnp.float32)
    outgoing, own_part = apply_blocks(nbr, position, latent_all, latent, gt, si, zero)
    returned = lax.all_to_all(
        outgoing.reshape(device_count, capacity, field_count, point_count),
        axes, split_axis=0, concat_axis=0, tiled=True,
    )
    asked_flat = kept.reshape(-1)
    selector = (asked_flat[None, :] == lax.broadcasted_iota(jnp.int32, (block_count, 1), 0)).astype(
        jnp.float32
    )
    summed = jnp.dot(
        selector,
        returned.reshape(device_count * capacity, field_count * point_count),
        precision=HI,
        preferred_element_type=jnp.float32,
    )
    prior = summed.reshape(block_count, field_count, point_count) + own_part
    eye = lax.broadcasted_iota(jnp.int32, (128, 128), 0) == lax.broadcasted_iota(jnp.int32, (128, 128), 1)
    qdiag = jnp.sum(jnp.where(eye, si, 0.0), axis=1)
    sign = 2.0 * labels.astype(jnp.float32) - 1.0
    margin = sign * latent
    ratio = probit_ratio(margin)
    weight = ratio * (ratio + margin)
    delta = (sign * ratio - prior) / (weight + qdiag[:, None, :])
    spread = lax.psum(jnp.sum(delta * delta, axis=(0, 2)), axes)
    step_rms = jnp.sqrt(spread / (block_count * point_count * device_count) + 1e-06)
    new_latent = latent + 0.5 * delta / step_rms[None, :, None]
    return (new_latent, step_rms)


def solution(mesh):
    both = ("blk", "nb")
    return jax.shard_map(
        body,
        mesh=mesh,
        in_specs=(P(both, None, None), P(both, None, None), P(both, None, None), P(both, None), P(both, None)),
        out_specs=(P(both, None, None), P()),
        check_vma=False,
    )
```

```python
import math
import functools
import jax
import jax.numpy as jnp
from jax import lax
from jax.experimental import pallas as pl
from jax.experimental.pallas import tpu as pltpu
from jax.sharding import PartitionSpec as P

nugget = 0.25
length_scale = 0.1
NN = (((1,), (0,)), ((), ()))
NT = (((1,), (1,)), ((), ()))
TN = (((0,), (0,)), ((), ()))


def split(x):
    high = x.astype(jnp.bfloat16)
    return high, (x - high.astype(jnp.float32)).astype(jnp.bfloat16)


def dot(a, b, dims):
    return lax.dot_general(a, b, dims, preferred_element_type=jnp.float32)


def wide(a, b, dims=NN):
    ca, cb = dims[0][0][0], dims[0][1][0]
    left = jnp.concatenate([a[0], a[1], a[0]], axis=ca)
    right = jnp.concatenate([b[0], b[0], b[1]], axis=cb)
    return dot(left, right, dims)


def small(a, b, dims=NN):
    return dot(a[0], b[0], dims) + (dot(a[0], b[1], dims) + dot(a[1], b[0], dims))


def eliminate(packs):
    lane = lax.broadcasted_iota(jnp.int32, (8, 128), 1)
    row = lax.broadcasted_iota(jnp.int32, (8, 128), 0)
    base = lane & 64
    inner = lane & 63
    for section in range(8):
        def step(t, carry, section=section):
            sub = 2 * t
            p = 8 * section + sub
            at0 = base + p
            at1 = at0 + 1
            first = inner == p
            second = inner == p + 1
            own = first | second
            below = row > sub + 1
            for pack in packs:
                x0 = pack[8 * section:8 * section + 8, :]
                r1 = jnp.broadcast_to(pack[pl.ds(p, 1), :], (8, 128))
                r2 = jnp.broadcast_to(pack[pl.ds(p + 1, 1), :], (8, 128))
                a = jnp.take_along_axis(r1, at0, axis=1)
                b = jnp.take_along_axis(r1, at1, axis=1)
                d = jnp.take_along_axis(r2, at1, axis=1)
                det = a * d - b * b
                rdet = 1.0 / det
                r1 = jnp.where(first, 1.0, jnp.where(second, 0.0, r1))
                r2 = jnp.where(first, 0.0, jnp.where(second, 1.0, r2))
                new1 = (d * r1 - b * r2) * rdet
                new2 = (a * r2 - b * r1) * rdet
                ra = lax.rsqrt(a)
                done1 = r1 * ra
                done2 = new2 * (det * (ra * lax.rsqrt(det)))
                c1 = jnp.take_along_axis(x0, at0, axis=1)
                c2 = jnp.take_along_axis(x0, at1, axis=1)
                x = jnp.where(own, 0.0, x0) - c1 * new1 - c2 * new2
                x = jnp.where(below, x, x0)
                x = jnp.where(row == sub, done1, jnp.where(row == sub + 1, done2, x))
                pack[8 * section:8 * section + 8, :] = x
                for s in range(section + 1, 8):
                    y = pack[8 * s:8 * s + 8, :]
                    c1 = jnp.take_along_axis(y, at0, axis=1)
                    c2 = jnp.take_along_axis(y, at1, axis=1)
                    pack[8 * s:8 * s + 8, :] = jnp.where(own, 0.0, y) - c1 * new1 - c2 * new2
            return carry

        lax.fori_loop(0, 4, step, 0)


def lower64(x):
    keep = lax.broadcasted_iota(jnp.int32, (64, 64), 0) >= lax.broadcasted_iota(jnp.int32, (64, 64), 1)
    return jnp.where(keep, x, 0.0)


def factor_kernel(owner_ref, slot_ref, coords_ref, own_ref, gt_ref, li_ref, qd_ref, cov, wh, wl, linv, *packs):
    n = own_ref.shape[0]
    near = owner_ref.shape[1]
    nt = near + 1
    last = near * 128
    scale = math.sqrt(3.0) / length_scale

    def build(m, carry):
        pts = [
            [coords_ref[owner_ref[m, k], pl.ds(2 * slot_ref[m, k] + i, 1), :] * scale for i in range(2)]
            for k in range(near)
        ] + [[own_ref[m, i:i + 1] * scale for i in range(2)]]
        for i in range(nt):
            xc = jnp.broadcast_to(pts[i][0], (128, 128)).T
            yc = jnp.broadcast_to(pts[i][1], (128, 128)).T
            for j in range(i + 1):
                dx = xc - pts[j][0]
                dy = yc - pts[j][1]
                q = dx * dx + dy * dy
                s = q * lax.rsqrt(jnp.maximum(q, 1e-30))
                c = (1.0 + s) * jnp.exp(-s)
                if i == j:
                    diag = lax.broadcasted_iota(jnp.int32, (128, 128), 0) == lax.broadcasted_iota(
                        jnp.int32, (128, 128), 1
                    )
                    c = c + jnp.where(diag, nugget, 0.0)
                cov[m, i * 128:(i + 1) * 128, j * 128:(j + 1) * 128] = c
        return carry

    lax.fori_loop(0, n, build, 0)

    def terms(ref_h, ref_l, *at):
        return ref_h[at], ref_l[at]

    for j in range(nt):
        lo, hi = j * 128, (j + 1) * 128
        rows = slice(lo, hi)

        if j:
            def left(m, carry):
                a = (wh[m, lo:, :lo], wl[m, lo:, :lo])
                b = (wh[m, lo:hi, :lo], wl[m, lo:hi, :lo])
                cov[m, lo:, lo:hi] = cov[m, lo:, lo:hi] - wide(a, b, NT)
                return carry

            lax.fori_loop(0, n, left, 0)

        for m in range(n):
            packs[m // 2][:, (m % 2) * 64:(m % 2) * 64 + 64] = cov[m, lo:lo + 64, lo:lo + 64]
        eliminate(packs)
        for m in range(n):
            at = (m % 2) * 64
            top = split(lower64(packs[m // 2][:, at:at + 64]))
            w = split(small(split(cov[m, lo + 64:hi, lo:lo + 64]), top, NT))
            linv[j, m, 0:64, 0:64] = top[0].astype(jnp.float32) + top[1].astype(jnp.float32)
            linv[j, m, 0:64, 64:128] = jnp.zeros((64, 64), jnp.float32)
            linv[j, m, 64:128, 0:64] = small(w, top)
            linv[j, m, 64:128, 64:128] = cov[m, lo + 64:hi, lo + 64:hi] - small(w, w, NT)
        for m in range(n):
            packs[m // 2][:, (m % 2) * 64:(m % 2) * 64 + 64] = linv[j, m, 64:128, 64:128]
        eliminate(packs)
        for m in range(n):
            at = (m % 2) * 64
            low = lower64(packs[m // 2][:, at:at + 64])
            linv[j, m, 64:128, 64:128] = low
            linv[j, m, 64:128, 0:64] = -small(split(low), split(linv[j, m, 64:128, 0:64]))

        if j < near:
            def panel(m, carry):
                w = split(wide(split(cov[m, hi:, lo:hi]), split(linv[j, m]), NT))
                wh[m, hi:, lo:hi] = w[0]
                wl[m, hi:, lo:hi] = w[1]
                return carry

            lax.fori_loop(0, n, panel, 0)

    def back(m, carry):
        for k in reversed(range(near)):
            lo, hi = k * 128, (k + 1) * 128
            g = wh[m, last:, lo:hi].astype(jnp.float32) + wl[m, last:, lo:hi].astype(jnp.float32)
            if hi < last:
                g = g - wide(split(gt_ref[m, :, hi:last]), (wh[m, hi:last, lo:hi], wl[m, hi:last, lo:hi]))
            gt_ref[m, :, lo:hi] = wide(split(g), split(linv[k, m]))
        li = linv[near, m]
        li_ref[m] = li
        qd_ref[m] = jnp.sum(li * li, axis=0, keepdims=True)
        return carry

    lax.fori_loop(0, n, back, 0)


def factor(owner, slot, coords_all, coords_own):
    n, near = owner.shape
    width = (near + 1) * 128
    return pl.pallas_call(
        factor_kernel,
        out_shape=(
            jax.ShapeDtypeStruct((n, 128, near * 128), jnp.float32),
            jax.ShapeDtypeStruct((n, 128, 128), jnp.float32),
            jax.ShapeDtypeStruct((n, 1, 128), jnp.float32),
        ),
        in_specs=[pl.BlockSpec(memory_space=pltpu.SMEM)] * 2 + [pl.BlockSpec(memory_space=pltpu.VMEM)] * 2,
        out_specs=(pl.BlockSpec(memory_space=pltpu.VMEM),) * 3,
        scratch_shapes=[
            pltpu.VMEM((n, width, width), jnp.float32),
            pltpu.VMEM((n, width, width - 128), jnp.bfloat16),
            pltpu.VMEM((n, width, width - 128), jnp.bfloat16),
            pltpu.VMEM((near + 1, n, 128, 128), jnp.float32),
        ]
        + [pltpu.VMEM((64, 128), jnp.float32)] * (n // 2),
        compiler_params=pltpu.CompilerParams(vmem_limit_bytes=56 * 1024 * 1024),
        cost_estimate=pl.CostEstimate(flops=2_000_000_000, bytes_accessed=5_000_000, transcendentals=4_000_000),
        name="factor",
    )(owner, slot, coords_all, coords_own)


MESH = pl.DeviceIdType.MESH
SIDE = 4


def place():
    blk, y = lax.axis_index("blk"), lax.axis_index("nb")
    return {"z": blk // (2 * SIDE), "x": lax.rem(blk // 2, SIDE), "c": lax.rem(blk, 2), "y": y}


def device(at, **moved):
    to = {**at, **moved}
    return (to["z"] * (2 * SIDE) + to["x"] * 2 + to["c"], to["y"])


def ahead(at, axis, k):
    return lax.rem(at[axis] + k, SIDE)


def meet(partners):
    barrier = pltpu.get_barrier_semaphore()
    for partner in partners:
        pl.semaphore_signal(barrier, inc=1, device_id=partner, device_id_type=MESH)
    pl.semaphore_wait(barrier, len(partners))


def everywhere_kernel(x_ref, out_ref, own_sem, send, recv):
    at = place()
    near = [(axis, k) for axis in "yxz" for k in range(1, SIDE)]
    partners = [device(at, **{axis: ahead(at, axis, k)}) for axis, k in near] + [device(at, c=1 - at["c"])]
    own = pltpu.make_async_copy(x_ref, out_ref.at[at["z"], at["x"], at["c"], at["y"]], own_sem)
    own.start()
    meet(partners)

    def push(src, i):
        return pltpu.make_async_remote_copy(
            src_ref=src[0], dst_ref=src[1], send_sem=send.at[i], recv_sem=recv.at[i],
            device_id=partners[i], device_id_type=MESH,
        )

    line = out_ref.at[at["z"], at["x"], at["c"], at["y"]]
    stages = [
        [push((x_ref, line), i) for i in range(0, 3)],
        [push((out_ref.at[at["z"], at["x"], at["c"]],) * 2, i) for i in range(3, 6)],
        [push((out_ref.at[at["z"], :, at["c"]],) * 2, i) for i in range(6, 9)],
        [push((out_ref.at[:, :, at["c"]],) * 2, 9)],
    ]
    for number, stage in enumerate(stages):
        if number == 1:
            own.wait()
        for copy in stage:
            copy.start()
        for copy in stage:
            copy.wait_recv()
    for stage in stages:
        for copy in stage:
            copy.wait_send()


def everywhere(x, collective_id):
    out = pl.pallas_call(
        everywhere_kernel,
        out_shape=jax.ShapeDtypeStruct((SIDE, SIDE, 2, SIDE) + x.shape, x.dtype),
        in_specs=[pl.BlockSpec(memory_space=pltpu.VMEM)],
        out_specs=pl.BlockSpec(memory_space=pltpu.VMEM),
        scratch_shapes=[
            pltpu.SemaphoreType.DMA(()),
            pltpu.SemaphoreType.DMA((10,)),
            pltpu.SemaphoreType.DMA((10,)),
        ],
        compiler_params=pltpu.CompilerParams(collective_id=collective_id, has_side_effects=True),
        name="everywhere",
    )(x)
    return out.reshape((2 * SIDE ** 3,) + x.shape)


def apply_kernel(nbr_ref, pos_ref, v0_ref, v1_ref, v2_ref, v3_ref, own_ref, gt_ref, li_ref, zero_ref, out_ref, u_ref, keep):
    k = pl.program_id(1)

    @pl.when(k == 0)
    def _():
        r = own_ref[0]
        for i, v in enumerate((v0_ref, v1_ref, v2_ref, v3_ref)):
            r = r - wide(split(v[0]), split(gt_ref[0, :, i * 128:(i + 1) * 128]), NT)
        u = wide(split(wide(split(r), split(li_ref[0]), NT)), split(li_ref[0]))
        keep[...] = u
        u_ref[0] = u

    g = gt_ref[0, :, pl.ds(pl.multiple_of(k * 128, 128), 128)]
    out_ref[0] = -wide(split(keep[...]), split(g))


def apply_blocks(nbr, pos, latent_all, latent, gt, si, zero):
    n, near = nbr.shape
    fields = latent.shape[1]
    def v_spec(i):
        return pl.BlockSpec((1, fields, 128), lambda b, k, nbr, pos: (nbr[b * near + i], 0, 0))
    def b_spec(*shape):
        return pl.BlockSpec((1,) + shape, lambda b, k, nbr, pos: (b, 0, 0))
    return pl.pallas_call(
        apply_kernel,
        out_shape=(
            jax.ShapeDtypeStruct(zero.shape, jnp.float32),
            jax.ShapeDtypeStruct(latent.shape, jnp.float32),
        ),
        grid_spec=pltpu.PrefetchScalarGridSpec(
            num_scalar_prefetch=2,
            grid=(n, near),
            in_specs=[v_spec(i) for i in range(near)]
            + [b_spec(fields, 128), b_spec(128, near * 128), b_spec(128, 128), pl.BlockSpec(memory_space=pl.ANY)],
            out_specs=(
                pl.BlockSpec((1, fields, 128), lambda b, k, nbr, pos: (pos[b * near + k], 0, 0)),
                b_spec(fields, 128),
            ),
            scratch_shapes=[pltpu.VMEM((fields, 128), jnp.float32)],
        ),
        input_output_aliases={9: 0},
        name="apply",
    )(nbr.reshape(-1), pos.reshape(-1), *([latent_all] * near), latent, gt, si, zero)


def probit_ratio(margin):
    density = jnp.exp(-0.5 * margin * margin - 0.5 * math.log(2.0 * math.pi))
    mass = 0.5 * lax.erfc(-margin / math.sqrt(2.0))
    return density / mass


def body(latent, coords, labels, owner, slot):
    block_count, field_count, point_count = latent.shape
    near_count = owner.shape[1]
    axes = ("blk", "nb")
    device_count = lax.axis_size("blk") * lax.axis_size("nb")
    capacity = max(2, 2 * block_count * near_count // device_count)
    nbr = owner * block_count + slot
    coords_all = everywhere(coords.reshape(2 * block_count, point_count), 1)
    latent_all = lax.all_gather(latent, axes, axis=0, tiled=True)
    wanted = owner.reshape(-1)
    places = slot.reshape(-1)
    request_count = wanted.shape[0]
    earlier = lax.broadcasted_iota(
        jnp.int32, (request_count, request_count), 1
    ) < lax.broadcasted_iota(jnp.int32, (request_count, request_count), 0)
    slot_rank = jnp.sum(
        jnp.where((wanted[None, :] == wanted[:, None]) & earlier, 1, 0), axis=1
    ).astype(jnp.int32)
    position = wanted * capacity + slot_rank
    requests = jnp.full((device_count * capacity,), -1, jnp.int32).at[position].set(places)
    kept = lax.all_to_all(
        requests.reshape(device_count, capacity), axes, split_axis=0, concat_axis=0, tiled=True
    )
    gt, li, qdiag = factor(owner, slot, coords_all, coords)
    zero = jnp.zeros((device_count * capacity, field_count, point_count), jnp.float32)
    outgoing, own_part = apply_blocks(nbr, position, latent_all, latent, gt, li, zero)
    returned = lax.all_to_all(
        outgoing.reshape(device_count, capacity, field_count, point_count),
        axes, split_axis=0, concat_axis=0, tiled=True,
    )
    asked_flat = kept.reshape(-1)
    selector = (asked_flat[None, :] == lax.broadcasted_iota(jnp.int32, (block_count, 1), 0)).astype(
        jnp.float32
    )
    summed = jnp.dot(
        selector,
        returned.reshape(device_count * capacity, field_count * point_count),
        precision=lax.Precision.HIGHEST,
        preferred_element_type=jnp.float32,
    )
    prior = summed.reshape(block_count, field_count, point_count) + own_part
    sign = 2.0 * labels.astype(jnp.float32) - 1.0
    margin = sign * latent
    ratio = probit_ratio(margin)
    weight = ratio * (ratio + margin)
    delta = (sign * ratio - prior) / (weight + qdiag)
    partial = jnp.sum(delta * delta, axis=(0, 2))
    spread = jnp.sum(everywhere(jnp.pad(partial, (0, 128 - field_count))[None], 2), axis=(0, 1))[:field_count]
    step_rms = jnp.sqrt(spread / (block_count * point_count * device_count) + 1e-06)
    new_latent = latent + 0.5 * delta / step_rms[None, :, None]
    return (new_latent, step_rms)


def solution(mesh):
    both = ("blk", "nb")
    return jax.shard_map(
        body,
        mesh=mesh,
        in_specs=(P(both, None, None), P(both, None, None), P(both, None, None), P(both, None), P(both, None)),
        out_specs=(P(both, None, None), P()),
        check_vma=False,
    )
```

```python
import math
import functools
import jax
import jax.numpy as jnp
from jax import lax
from jax.experimental import pallas as pl
from jax.experimental.pallas import tpu as pltpu
from jax.sharding import PartitionSpec as P

nugget = 0.25
length_scale = 0.1
NN = (((1,), (0,)), ((), ()))
NT = (((1,), (1,)), ((), ()))
TN = (((0,), (0,)), ((), ()))


def split(x):
    high = x.astype(jnp.bfloat16)
    return high, (x - high.astype(jnp.float32)).astype(jnp.bfloat16)


def dot(a, b, dims):
    return lax.dot_general(a, b, dims, preferred_element_type=jnp.float32)


def wide(a, b, dims=NN):
    ca, cb = dims[0][0][0], dims[0][1][0]
    left = jnp.concatenate([a[0], a[1], a[0]], axis=ca)
    right = jnp.concatenate([b[0], b[0], b[1]], axis=cb)
    return dot(left, right, dims)


def small(a, b, dims=NN):
    return dot(a[0], b[0], dims) + (dot(a[0], b[1], dims) + dot(a[1], b[0], dims))


def eliminate(packs):
    lane = lax.broadcasted_iota(jnp.int32, (8, 128), 1)
    row = lax.broadcasted_iota(jnp.int32, (8, 128), 0)
    base = lane & 64
    inner = lane & 63

    def pick(x, at):
        return jnp.take_along_axis(x, at, axis=1)

    for p in range(0, 64, 2):
        top, sub = p // 8, p % 8
        at0, at1 = base + p, base + (p + 1)
        first, second = inner == p, inner == p + 1
        own = first | second
        lead = []
        for pack in packs:
            r1 = jnp.broadcast_to(pack[p:p + 1, :], (8, 128))
            r2 = jnp.broadcast_to(pack[p + 1:p + 2, :], (8, 128))
            lead.append((r1, r2, pick(r1, at0), pick(r1, at1), pick(r2, at1)))
        news = []
        for r1, r2, a, b, d in lead:
            det = a * d - b * b
            rdet = 1.0 / det
            r1 = jnp.where(first, 1.0, jnp.where(second, 0.0, r1))
            r2 = jnp.where(first, 0.0, jnp.where(second, 1.0, r2))
            new1 = (d * r1 - b * r2) * rdet
            new2 = (a * r2 - b * r1) * rdet
            ra = lax.rsqrt(a)
            news.append((new1, new2, r1 * ra, new2 * (det * (ra * lax.rsqrt(det)))))
        for pack, (new1, new2, done1, done2) in zip(packs, news):
            for s in range(top, 8):
                y = pack[8 * s:8 * s + 8, :]
                x = jnp.where(own, 0.0, y) - pick(y, at0) * new1 - pick(y, at1) * new2
                if s == top:
                    x = jnp.where(row > sub + 1, x, jnp.where(row == sub, done1, jnp.where(row == sub + 1, done2, y)))
                pack[8 * s:8 * s + 8, :] = x


def lower64(x):
    keep = lax.broadcasted_iota(jnp.int32, (64, 64), 0) >= lax.broadcasted_iota(jnp.int32, (64, 64), 1)
    return jnp.where(keep, x, 0.0)


def factor_kernel(owner_ref, slot_ref, coords_ref, own_ref, gt_ref, li_ref, qd_ref, cov, wh, wl, linv, *packs):
    n = own_ref.shape[0]
    near = owner_ref.shape[1]
    nt = near + 1
    last = near * 128
    scale = math.sqrt(3.0) / length_scale

    def build(m, carry):
        pts = [
            [coords_ref[owner_ref[m, k], pl.ds(2 * slot_ref[m, k] + i, 1), :] * scale for i in range(2)]
            for k in range(near)
        ] + [[own_ref[m, i:i + 1] * scale for i in range(2)]]
        for i in range(nt):
            xc = jnp.broadcast_to(pts[i][0], (128, 128)).T
            yc = jnp.broadcast_to(pts[i][1], (128, 128)).T
            for j in range(i + 1):
                dx = xc - pts[j][0]
                dy = yc - pts[j][1]
                q = dx * dx + dy * dy
                s = q * lax.rsqrt(jnp.maximum(q, 1e-30))
                c = (1.0 + s) * jnp.exp(-s)
                if i == j:
                    diag = lax.broadcasted_iota(jnp.int32, (128, 128), 0) == lax.broadcasted_iota(
                        jnp.int32, (128, 128), 1
                    )
                    c = c + jnp.where(diag, nugget, 0.0)
                cov[m, i * 128:(i + 1) * 128, j * 128:(j + 1) * 128] = c
        return carry

    lax.fori_loop(0, n, build, 0)

    def terms(ref_h, ref_l, *at):
        return ref_h[at], ref_l[at]

    for j in range(nt):
        lo, hi = j * 128, (j + 1) * 128
        rows = slice(lo, hi)

        if j:
            def left(m, carry):
                a = (wh[m, lo:, :lo], wl[m, lo:, :lo])
                b = (wh[m, lo:hi, :lo], wl[m, lo:hi, :lo])
                cov[m, lo:, lo:hi] = cov[m, lo:, lo:hi] - wide(a, b, NT)
                return carry

            lax.fori_loop(0, n, left, 0)

        for m in range(n):
            packs[m // 2][:, (m % 2) * 64:(m % 2) * 64 + 64] = cov[m, lo:lo + 64, lo:lo + 64]
        eliminate(packs)
        for m in range(n):
            at = (m % 2) * 64
            top = split(lower64(packs[m // 2][:, at:at + 64]))
            w = split(small(split(cov[m, lo + 64:hi, lo:lo + 64]), top, NT))
            linv[j, m, 0:64, 0:64] = top[0].astype(jnp.float32) + top[1].astype(jnp.float32)
            linv[j, m, 0:64, 64:128] = jnp.zeros((64, 64), jnp.float32)
            linv[j, m, 64:128, 0:64] = small(w, top)
            linv[j, m, 64:128, 64:128] = cov[m, lo + 64:hi, lo + 64:hi] - small(w, w, NT)
        for m in range(n):
            packs[m // 2][:, (m % 2) * 64:(m % 2) * 64 + 64] = linv[j, m, 64:128, 64:128]
        eliminate(packs)
        for m in range(n):
            at = (m % 2) * 64
            low = lower64(packs[m // 2][:, at:at + 64])
            linv[j, m, 64:128, 64:128] = low
            linv[j, m, 64:128, 0:64] = -small(split(low), split(linv[j, m, 64:128, 0:64]))

        if j < near:
            def panel(m, carry):
                w = split(wide(split(cov[m, hi:, lo:hi]), split(linv[j, m]), NT))
                wh[m, hi:, lo:hi] = w[0]
                wl[m, hi:, lo:hi] = w[1]
                return carry

            lax.fori_loop(0, n, panel, 0)

    def back(m, carry):
        for k in reversed(range(near)):
            lo, hi = k * 128, (k + 1) * 128
            g = wh[m, last:, lo:hi].astype(jnp.float32) + wl[m, last:, lo:hi].astype(jnp.float32)
            if hi < last:
                g = g - wide(split(gt_ref[m, :, hi:last]), (wh[m, hi:last, lo:hi], wl[m, hi:last, lo:hi]))
            gt_ref[m, :, lo:hi] = wide(split(g), split(linv[k, m]))
        li = linv[near, m]
        li_ref[m] = li
        qd_ref[m] = jnp.sum(li * li, axis=0, keepdims=True)
        return carry

    lax.fori_loop(0, n, back, 0)


def factor(owner, slot, coords_all, coords_own):
    n, near = owner.shape
    width = (near + 1) * 128
    return pl.pallas_call(
        factor_kernel,
        out_shape=(
            jax.ShapeDtypeStruct((n, 128, near * 128), jnp.float32),
            jax.ShapeDtypeStruct((n, 128, 128), jnp.float32),
            jax.ShapeDtypeStruct((n, 1, 128), jnp.float32),
        ),
        in_specs=[pl.BlockSpec(memory_space=pltpu.SMEM)] * 2 + [pl.BlockSpec(memory_space=pltpu.VMEM)] * 2,
        out_specs=(pl.BlockSpec(memory_space=pltpu.VMEM),) * 3,
        scratch_shapes=[
            pltpu.VMEM((n, width, width), jnp.float32),
            pltpu.VMEM((n, width, width - 128), jnp.bfloat16),
            pltpu.VMEM((n, width, width - 128), jnp.bfloat16),
            pltpu.VMEM((near + 1, n, 128, 128), jnp.float32),
        ]
        + [pltpu.VMEM((64, 128), jnp.float32)] * (n // 2),
        compiler_params=pltpu.CompilerParams(vmem_limit_bytes=56 * 1024 * 1024),
        cost_estimate=pl.CostEstimate(flops=2_000_000_000, bytes_accessed=5_000_000, transcendentals=4_000_000),
        name="factor",
    )(owner, slot, coords_all, coords_own)


MESH = pl.DeviceIdType.MESH
SIDE = 4


def place():
    blk, y = lax.axis_index("blk"), lax.axis_index("nb")
    return {"z": blk // (2 * SIDE), "x": lax.rem(blk // 2, SIDE), "c": lax.rem(blk, 2), "y": y}


def device(at, **moved):
    to = {**at, **moved}
    return (to["z"] * (2 * SIDE) + to["x"] * 2 + to["c"], to["y"])


def ahead(at, axis, k):
    return lax.rem(at[axis] + k, SIDE)


def meet(partners):
    barrier = pltpu.get_barrier_semaphore()
    for partner in partners:
        pl.semaphore_signal(barrier, inc=1, device_id=partner, device_id_type=MESH)
    pl.semaphore_wait(barrier, len(partners))


def everywhere_kernel(x_ref, out_ref, own_sem, send, recv):
    at = place()
    near = [(axis, k) for axis in "yxz" for k in range(1, SIDE)]
    partners = [device(at, **{axis: ahead(at, axis, k)}) for axis, k in near] + [device(at, c=1 - at["c"])]
    own = pltpu.make_async_copy(x_ref, out_ref.at[at["z"], at["x"], at["c"], at["y"]], own_sem)
    own.start()
    meet(partners)

    def push(src, i):
        return pltpu.make_async_remote_copy(
            src_ref=src[0], dst_ref=src[1], send_sem=send.at[i], recv_sem=recv.at[i],
            device_id=partners[i], device_id_type=MESH,
        )

    line = out_ref.at[at["z"], at["x"], at["c"], at["y"]]
    stages = [
        [push((x_ref, line), i) for i in range(0, 3)],
        [push((out_ref.at[at["z"], at["x"], at["c"]],) * 2, i) for i in range(3, 6)],
        [push((out_ref.at[at["z"], :, at["c"]],) * 2, i) for i in range(6, 9)],
        [push((out_ref.at[:, :, at["c"]],) * 2, 9)],
    ]
    for number, stage in enumerate(stages):
        if number == 1:
            own.wait()
        for copy in stage:
            copy.start()
        for copy in stage:
            copy.wait_recv()
    for stage in stages:
        for copy in stage:
            copy.wait_send()


def everywhere(x, collective_id):
    out = pl.pallas_call(
        everywhere_kernel,
        out_shape=jax.ShapeDtypeStruct((SIDE, SIDE, 2, SIDE) + x.shape, x.dtype),
        in_specs=[pl.BlockSpec(memory_space=pltpu.VMEM)],
        out_specs=pl.BlockSpec(memory_space=pltpu.VMEM),
        scratch_shapes=[
            pltpu.SemaphoreType.DMA(()),
            pltpu.SemaphoreType.DMA((10,)),
            pltpu.SemaphoreType.DMA((10,)),
        ],
        compiler_params=pltpu.CompilerParams(collective_id=collective_id, has_side_effects=True),
        name="everywhere",
    )(x)
    return out.reshape((2 * SIDE ** 3,) + x.shape)


ROUTES = (("x", "z", "y"), ("y", "x", "z"), ("z", "y", "x"))
CAP = 12


def coordinates(index):
    return {
        "z": index // (4 * SIDE * 2),
        "x": lax.rem(index // (2 * SIDE), SIDE),
        "c": lax.rem(index // SIDE, 2),
        "y": lax.rem(index, SIDE),
    }


def deal_kernel(*refs):
    count = len(ROUTES)
    data, meta = refs[:count], refs[count:2 * count]
    got, got_meta = refs[2 * count:3 * count], refs[3 * count:4 * count]
    own_sem, send, recv = refs[4 * count:]
    at = place()
    moves = [(k, j) for k in range(SIDE) for j in range(2) if k or j]
    partners, jobs = [], []
    for r, (axis, _, _) in enumerate(ROUTES):
        for k, j in moves:
            to = {axis: ahead(at, axis, k), "c": lax.rem(at["c"] + j, 2)}
            if k or r == 0:
                partners.append(device(at, **to))
            jobs.append((r, axis, to))
    local = []
    for r, (axis, _, _) in enumerate(ROUTES):
        for i, (src, dst) in enumerate(((data, got), (meta, got_meta))):
            here = (at[axis], at["c"])
            local.append(pltpu.make_async_copy(src[r].at[here], dst[r].at[here], own_sem.at[r, i]))
    for copy in local:
        copy.start()
    meet(partners)
    copies = []
    for n, (r, axis, to) in enumerate(jobs):
        for i, (src, dst) in enumerate(((data, got), (meta, got_meta))):
            copies.append(
                pltpu.make_async_remote_copy(
                    src_ref=src[r].at[to[axis], to["c"]],
                    dst_ref=dst[r].at[at[axis], at["c"]],
                    send_sem=send.at[n, i],
                    recv_sem=recv.at[n, i],
                    device_id=device(at, **to),
                    device_id_type=MESH,
                )
            )
    for copy in copies:
        copy.start()
    for copy in copies:
        copy.wait()
    for copy in local:
        copy.wait()


def deal(data, meta, collective_id):
    jobs = 7 * len(ROUTES)
    shapes = [jax.ShapeDtypeStruct(a.shape, a.dtype) for a in (*data, *meta)]
    out = pl.pallas_call(
        deal_kernel,
        out_shape=tuple(shapes),
        in_specs=[pl.BlockSpec(memory_space=pl.ANY)] * len(shapes),
        out_specs=(pl.BlockSpec(memory_space=pl.ANY),) * len(shapes),
        scratch_shapes=[
            pltpu.SemaphoreType.DMA((len(ROUTES), 2)),
            pltpu.SemaphoreType.DMA((jobs, 2)),
            pltpu.SemaphoreType.DMA((jobs, 2)),
        ],
        compiler_params=pltpu.CompilerParams(collective_id=collective_id, has_side_effects=True),
        name="deal",
    )(*data, *meta)
    return out[:len(ROUTES)], out[len(ROUTES):]


def pile_kernel(*refs):
    count = len(ROUTES)
    meta, got, dense = refs[:count], refs[count:2 * count], refs[2 * count:]
    g = pl.program_id(0)

    @pl.when(g == 0)
    def _():
        for d in dense:
            def clear(i, carry, d=d):
                d[pl.ds(8 * i, 8)] = jnp.zeros((8,) + d.shape[1:], jnp.float32)
                return carry

            lax.fori_loop(0, d.shape[0] // 8, clear, 0)

    for r in range(count):
        def add(i, carry, r=r):
            to = meta[r][g * 128 + i]
            dense[r][to] = dense[r][to] + got[r][0, i]
            return carry

        lax.fori_loop(0, meta[r][g * 128 + CAP], add, 0)


def pile(meta, got, places):
    count = len(ROUTES)
    rows = got[0].shape[-2]
    slab = pl.BlockSpec((1, CAP, rows, 128), lambda g, *m: (g, 0, 0, 0))
    whole = pl.BlockSpec((places, rows, 128), lambda g, *m: (0, 0, 0))
    return pl.pallas_call(
        pile_kernel,
        out_shape=(jax.ShapeDtypeStruct((places, rows, 128), jnp.float32),) * count,
        grid_spec=pltpu.PrefetchScalarGridSpec(
            num_scalar_prefetch=count,
            grid=(2 * SIDE,),
            in_specs=[slab] * count,
            out_specs=(whole,) * count,
        ),
        compiler_params=pltpu.CompilerParams(vmem_limit_bytes=40 * 1024 * 1024),
        name="pile",
    )(*[m.reshape(-1) for m in meta], *[a.reshape(2 * SIDE, CAP, rows, 128) for a in got])


def fold_kernel(*refs):
    count = len(ROUTES)
    dense, out, mine = refs[:count], refs[count], refs[count + 1:2 * count + 1]
    first, second = refs[2 * count + 1:3 * count + 1], refs[3 * count + 1:4 * count + 1]
    own_sem, send1, recv1, send2, recv2 = refs[4 * count + 1:]
    at = place()
    partners = [device(at, **{axis: ahead(at, axis, k)}) for axis in "xyz" for k in range(1, SIDE)]
    local = [
        pltpu.make_async_copy(dense[r].at[at[f]], mine[r], own_sem.at[r]) for r, (_, f, _) in enumerate(ROUTES)
    ]
    for copy in local:
        copy.start()
    meet(partners)

    def push(src, dst, send, recv, axis, k):
        return pltpu.make_async_remote_copy(
            src_ref=src, dst_ref=dst, send_sem=send, recv_sem=recv,
            device_id=device(at, **{axis: ahead(at, axis, k)}), device_id_type=MESH,
        )

    ones = [
        [
            push(dense[r].at[ahead(at, f, k)], first[r].at[k - 1], send1.at[r, k - 1], recv1.at[r, k - 1], f, k)
            for k in range(1, SIDE)
        ]
        for r, (_, f, _) in enumerate(ROUTES)
    ]
    for k in range(SIDE - 1):
        for r in range(count):
            ones[r][k].start()
    twos = []
    rows = first[0].shape[-2]
    for r, (_, f, s) in enumerate(ROUTES):
        local[r].wait()
        for copy in ones[r]:
            copy.wait_recv()
        mine[r][...] = (mine[r][...] + first[r][0]) + (first[r][1] + first[r][2])
        twos.append([
            push(mine[r].at[ahead(at, s, k)], second[r].at[k - 1], send2.at[r, k - 1], recv2.at[r, k - 1], s, k)
            for k in range(1, SIDE)
        ])
        for copy in twos[r]:
            copy.start()
    for r, (_, f, s) in enumerate(ROUTES):
        for copy in twos[r]:
            copy.wait_recv()
        out[:, r * rows:(r + 1) * rows, :] = (mine[r][at[s]] + second[r][0]) + (second[r][1] + second[r][2])
    for r in range(count):
        for copy in ones[r] + twos[r]:
            copy.wait_send()


def fold(dense, slots, collective_id):
    count = len(ROUTES)
    rows = dense[0].shape[-2]
    dense = [d.reshape(SIDE, SIDE, slots, rows, 128) for d in dense]
    part = (SIDE, slots, rows, 128)
    return pl.pallas_call(
        fold_kernel,
        out_shape=jax.ShapeDtypeStruct((slots, count * rows, 128), jnp.float32),
        in_specs=[pl.BlockSpec(memory_space=pl.ANY)] * count,
        out_specs=pl.BlockSpec(memory_space=pltpu.VMEM),
        scratch_shapes=[pltpu.VMEM(part, jnp.float32)] * count
        + [pltpu.VMEM((SIDE - 1,) + part, jnp.float32)] * count
        + [pltpu.VMEM((SIDE - 1,) + part[1:], jnp.float32)] * count
        + [pltpu.SemaphoreType.DMA((count,))]
        + [pltpu.SemaphoreType.DMA((count, SIDE - 1))] * 4,
        compiler_params=pltpu.CompilerParams(
            collective_id=collective_id, has_side_effects=True, vmem_limit_bytes=40 * 1024 * 1024
        ),
        name="fold",
    )(*dense)


def apply_kernel(outs, *refs):
    refs = refs[1 + outs:]
    near, (own_ref, gt_ref, li_ref) = refs[:-6 - outs + 1], refs[-5 - outs:-2 - outs]
    out_refs, u_ref, keep = refs[-2 - outs:-2], refs[-2], refs[-1]
    k = pl.program_id(1)

    @pl.when(k == 0)
    def _():
        r = own_ref[0]
        for i, v in enumerate(near):
            r = r - wide(split(v[0]), split(gt_ref[0, :, i * 128:(i + 1) * 128]), NT)
        low = split(li_ref[0])
        u = wide(split(wide(split(r), low, NT)), low)
        keep[...] = u
        u_ref[0] = u

    g = gt_ref[0, :, pl.ds(pl.multiple_of(k * 128, 128), 128)]
    pulled = -wide(split(keep[...]), split(g))
    rows = pulled.shape[0] // outs
    for i, out in enumerate(out_refs):
        out[0] = pulled[i * rows:(i + 1) * rows]


def apply_blocks(nbr, positions, length, latent_all, latent, gt, li):
    n, near = nbr.shape
    fields = latent.shape[1]
    outs = len(positions)
    rows = fields // outs

    def v_spec(i):
        return pl.BlockSpec((1, fields, 128), lambda b, k, nbr, *pos: (nbr[b * near + i], 0, 0))

    def b_spec(*shape):
        return pl.BlockSpec((1,) + shape, lambda b, k, *at: (b, 0, 0))

    def o_spec(i):
        return pl.BlockSpec((1, rows, 128), lambda b, k, nbr, *pos: (pos[i][b * near + k], 0, 0))

    return pl.pallas_call(
        functools.partial(apply_kernel, outs),
        out_shape=(jax.ShapeDtypeStruct((length, rows, 128), jnp.float32),) * outs
        + (jax.ShapeDtypeStruct(latent.shape, jnp.float32),),
        grid_spec=pltpu.PrefetchScalarGridSpec(
            num_scalar_prefetch=1 + outs,
            grid=(n, near),
            in_specs=[v_spec(i) for i in range(near)]
            + [b_spec(fields, 128), b_spec(128, near * 128), b_spec(128, 128)],
            out_specs=tuple(o_spec(i) for i in range(outs)) + (b_spec(fields, 128),),
            scratch_shapes=[pltpu.VMEM((fields, 128), jnp.float32)],
        ),
        name="apply",
    )(nbr.reshape(-1), *[p.reshape(-1) for p in positions], *([latent_all] * near), latent, gt, li)


def probit_ratio(margin):
    density = jnp.exp(-0.5 * margin * margin - 0.5 * math.log(2.0 * math.pi))
    mass = 0.5 * lax.erfc(-margin / math.sqrt(2.0))
    return density / mass


def rank_of(keys):
    count = keys.shape[0]
    earlier = lax.broadcasted_iota(jnp.int32, (count, count), 1) < lax.broadcasted_iota(
        jnp.int32, (count, count), 0
    )
    return jnp.sum(jnp.where((keys[None, :] == keys[:, None]) & earlier, 1, 0), axis=1).astype(jnp.int32)


def body(latent, coords, labels, owner, slot):
    block_count, field_count, point_count = latent.shape
    near_count = owner.shape[1]
    axes = ("blk", "nb")
    device_count = lax.axis_size("blk") * lax.axis_size("nb")
    nbr = owner * block_count + slot
    wanted = owner.reshape(-1)
    places = slot.reshape(-1)
    lies = coordinates(wanted)
    positions, metas, most = [], [], 0
    for sparse, one, two in ROUTES:
        group = lies[sparse] * 2 + lies["c"]
        rank = rank_of(group)
        most = jnp.maximum(most, jnp.max(rank))
        to = (lies[one] * SIDE + lies[two]) * block_count + places
        inside = jnp.minimum(rank, CAP - 1)
        lane = lax.broadcasted_iota(jnp.int32, (2 * SIDE, 128, 1), 1)
        which = lax.broadcasted_iota(jnp.int32, (2 * SIDE, 128, 1), 0)
        here = (which == group) & (lane == rank)
        total = jnp.sum(jnp.where(which == group, 1, 0), axis=2)
        meta = jnp.sum(jnp.where(here, to, 0), axis=2)
        meta = jnp.where(lane[:, :, 0] == CAP, total, meta)
        positions.append(group * CAP + inside)
        metas.append(meta.astype(jnp.int32).reshape(SIDE, 2, 1, 128))
    flag = jnp.where(most >= CAP, 1.0, 0.0).astype(jnp.float32)
    note = jnp.concatenate([coords.reshape(2 * block_count, point_count), jnp.full((8, point_count), flag)])
    notes = everywhere(note, 1)
    crowded = jnp.max(notes[:, 2 * block_count, :]) > 0.0
    latent_all = lax.all_gather(latent, axes, axis=0, tiled=True)
    gt, li, qdiag = factor(owner, slot, notes, coords)

    def routed():
        length = 2 * SIDE * CAP
        *data, own_part = apply_blocks(nbr, positions, length, latent_all, latent, gt, li)
        rows = field_count // len(ROUTES)
        got, got_meta = deal([d.reshape(SIDE, 2, CAP, rows, point_count) for d in data], metas, 3)
        dense = pile(got_meta, got, SIDE * SIDE * block_count)
        return own_part + fold(dense, block_count, 4)

    def padded():
        capacity = max(2, 2 * block_count * near_count // device_count)
        position = wanted * capacity + rank_of(wanted)
        requests = jnp.full((device_count * capacity,), -1, jnp.int32).at[position].set(places)
        asked = lax.all_to_all(
            requests.reshape(device_count, capacity), axes, split_axis=0, concat_axis=0, tiled=True
        ).reshape(-1)
        outgoing, own_part = apply_blocks(nbr, [position], device_count * capacity, latent_all, latent, gt, li)
        returned = lax.all_to_all(
            outgoing.reshape(device_count, capacity, field_count, point_count),
            axes, split_axis=0, concat_axis=0, tiled=True,
        ).reshape(device_count * capacity, field_count, point_count)
        returned = jnp.where((asked >= 0)[:, None, None], returned, 0.0)
        return own_part.at[jnp.maximum(asked, 0)].add(returned)

    prior = lax.cond(crowded, padded, routed)
    sign = 2.0 * labels.astype(jnp.float32) - 1.0
    margin = sign * latent
    ratio = probit_ratio(margin)
    weight = ratio * (ratio + margin)
    delta = (sign * ratio - prior) / (weight + qdiag)
    partial = jnp.sum(delta * delta, axis=(0, 2))
    spread = jnp.sum(everywhere(jnp.pad(partial, (0, 128 - field_count))[None], 2), axis=(0, 1))[:field_count]
    step_rms = jnp.sqrt(spread / (block_count * point_count * device_count) + 1e-06)
    new_latent = latent + 0.5 * delta / step_rms[None, :, None]
    return (new_latent, step_rms)


def solution(mesh):
    both = ("blk", "nb")
    return jax.shard_map(
        body,
        mesh=mesh,
        in_specs=(P(both, None, None), P(both, None, None), P(both, None, None), P(both, None), P(both, None)),
        out_specs=(P(both, None, None), P()),
        check_vma=False,
    )
```

```python
import math
import functools
import jax
import jax.numpy as jnp
from jax import lax
from jax.experimental import pallas as pl
from jax.experimental.pallas import tpu as pltpu
from jax.sharding import PartitionSpec as P

nugget = 0.25
length_scale = 0.1
NN = (((1,), (0,)), ((), ()))
NT = (((1,), (1,)), ((), ()))
TN = (((0,), (0,)), ((), ()))


def split(x):
    high = x.astype(jnp.bfloat16)
    return high, (x - high.astype(jnp.float32)).astype(jnp.bfloat16)


def dot(a, b, dims):
    return lax.dot_general(a, b, dims, preferred_element_type=jnp.float32)


def wide(a, b, dims=NN):
    ca, cb = dims[0][0][0], dims[0][1][0]
    left = jnp.concatenate([a[0], a[1], a[0]], axis=ca)
    right = jnp.concatenate([b[0], b[0], b[1]], axis=cb)
    return dot(left, right, dims)


def small(a, b, dims=NN):
    return dot(a[0], b[0], dims) + (dot(a[0], b[1], dims) + dot(a[1], b[0], dims))


def eliminate(packs):
    lane = lax.broadcasted_iota(jnp.int32, (8, 128), 1)
    row = lax.broadcasted_iota(jnp.int32, (8, 128), 0)
    base = lane & 64
    inner = lane & 63

    def pick(x, at):
        return jnp.take_along_axis(x, at, axis=1)

    for p in range(0, 64, 2):
        top, sub = p // 8, p % 8
        at0, at1 = base + p, base + (p + 1)
        first, second = inner == p, inner == p + 1
        own = first | second
        lead = []
        for pack in packs:
            r1 = jnp.broadcast_to(pack[p:p + 1, :], (8, 128))
            r2 = jnp.broadcast_to(pack[p + 1:p + 2, :], (8, 128))
            lead.append((r1, r2, pick(r1, at0), pick(r1, at1), pick(r2, at1)))
        news = []
        for r1, r2, a, b, d in lead:
            det = a * d - b * b
            rdet = 1.0 / det
            r1 = jnp.where(first, 1.0, jnp.where(second, 0.0, r1))
            r2 = jnp.where(first, 0.0, jnp.where(second, 1.0, r2))
            new1 = (d * r1 - b * r2) * rdet
            new2 = (a * r2 - b * r1) * rdet
            ra = lax.rsqrt(a)
            news.append((new1, new2, r1 * ra, new2 * (det * (ra * lax.rsqrt(det)))))
        for pack, (new1, new2, done1, done2) in zip(packs, news):
            for s in range(top, 8):
                y = pack[8 * s:8 * s + 8, :]
                x = jnp.where(own, 0.0, y) - pick(y, at0) * new1 - pick(y, at1) * new2
                if s == top:
                    x = jnp.where(row > sub + 1, x, jnp.where(row == sub, done1, jnp.where(row == sub + 1, done2, y)))
                pack[8 * s:8 * s + 8, :] = x


def lower64(x):
    keep = lax.broadcasted_iota(jnp.int32, (64, 64), 0) >= lax.broadcasted_iota(jnp.int32, (64, 64), 1)
    return jnp.where(keep, x, 0.0)


def factor_kernel(owner_ref, slot_ref, coords_ref, own_ref, gh_ref, gl_ref, lh_ref, ll_ref, qd_ref, cov, wh, wl, linv, *packs):
    n = own_ref.shape[0]
    near = owner_ref.shape[1]
    nt = near + 1
    last = near * 128
    scale = math.sqrt(3.0) / length_scale

    def build(m, carry):
        pts = [
            [coords_ref[owner_ref[m, k], pl.ds(2 * slot_ref[m, k] + i, 1), :] * scale for i in range(2)]
            for k in range(near)
        ] + [[own_ref[m, i:i + 1] * scale for i in range(2)]]
        for i in range(nt):
            xc = jnp.broadcast_to(pts[i][0], (128, 128)).T
            yc = jnp.broadcast_to(pts[i][1], (128, 128)).T
            for j in range(i + 1):
                dx = xc - pts[j][0]
                dy = yc - pts[j][1]
                q = dx * dx + dy * dy
                s = q * lax.rsqrt(jnp.maximum(q, 1e-30))
                c = (1.0 + s) * jnp.exp(-s)
                if i == j:
                    diag = lax.broadcasted_iota(jnp.int32, (128, 128), 0) == lax.broadcasted_iota(
                        jnp.int32, (128, 128), 1
                    )
                    c = c + jnp.where(diag, nugget, 0.0)
                cov[m, i * 128:(i + 1) * 128, j * 128:(j + 1) * 128] = c
        return carry

    lax.fori_loop(0, n, build, 0)

    def terms(ref_h, ref_l, *at):
        return ref_h[at], ref_l[at]

    for j in range(nt):
        lo, hi = j * 128, (j + 1) * 128
        rows = slice(lo, hi)

        if j:
            def left(m, carry):
                a = (wh[m, lo:, :lo], wl[m, lo:, :lo])
                b = (wh[m, lo:hi, :lo], wl[m, lo:hi, :lo])
                cov[m, lo:, lo:hi] = cov[m, lo:, lo:hi] - wide(a, b, NT)
                return carry

            lax.fori_loop(0, n, left, 0)

        for m in range(n):
            packs[m // 2][:, (m % 2) * 64:(m % 2) * 64 + 64] = cov[m, lo:lo + 64, lo:lo + 64]
        eliminate(packs)
        for m in range(n):
            at = (m % 2) * 64
            top = split(lower64(packs[m // 2][:, at:at + 64]))
            w = split(small(split(cov[m, lo + 64:hi, lo:lo + 64]), top, NT))
            linv[j, m, 0:64, 0:64] = top[0].astype(jnp.float32) + top[1].astype(jnp.float32)
            linv[j, m, 0:64, 64:128] = jnp.zeros((64, 64), jnp.float32)
            linv[j, m, 64:128, 0:64] = small(w, top)
            linv[j, m, 64:128, 64:128] = cov[m, lo + 64:hi, lo + 64:hi] - small(w, w, NT)
        for m in range(n):
            packs[m // 2][:, (m % 2) * 64:(m % 2) * 64 + 64] = linv[j, m, 64:128, 64:128]
        eliminate(packs)
        for m in range(n):
            at = (m % 2) * 64
            low = lower64(packs[m // 2][:, at:at + 64])
            linv[j, m, 64:128, 64:128] = low
            linv[j, m, 64:128, 0:64] = -small(split(low), split(linv[j, m, 64:128, 0:64]))

        if j < near:
            def panel(m, carry):
                w = split(wide(split(cov[m, hi:, lo:hi]), split(linv[j, m]), NT))
                wh[m, hi:, lo:hi] = w[0]
                wl[m, hi:, lo:hi] = w[1]
                return carry

            lax.fori_loop(0, n, panel, 0)

    def back(m, carry):
        for k in reversed(range(near)):
            lo, hi = k * 128, (k + 1) * 128
            g = wh[m, last:, lo:hi].astype(jnp.float32) + wl[m, last:, lo:hi].astype(jnp.float32)
            if hi < last:
                g = g - wide((gh_ref[m, :, hi:last], gl_ref[m, :, hi:last]), (wh[m, hi:last, lo:hi], wl[m, hi:last, lo:hi]))
            gh_ref[m, :, lo:hi], gl_ref[m, :, lo:hi] = split(wide(split(g), split(linv[k, m])))
        li = linv[near, m]
        lh_ref[m], ll_ref[m] = split(li)
        qd_ref[m] = jnp.sum(li * li, axis=0, keepdims=True)
        return carry

    lax.fori_loop(0, n, back, 0)


def factor(owner, slot, coords_all, coords_own):
    n, near = owner.shape
    width = (near + 1) * 128
    return pl.pallas_call(
        factor_kernel,
        out_shape=(jax.ShapeDtypeStruct((n, 128, near * 128), jnp.bfloat16),) * 2
        + (jax.ShapeDtypeStruct((n, 128, 128), jnp.bfloat16),) * 2
        + (jax.ShapeDtypeStruct((n, 1, 128), jnp.float32),),
        in_specs=[pl.BlockSpec(memory_space=pltpu.SMEM)] * 2 + [pl.BlockSpec(memory_space=pltpu.VMEM)] * 2,
        out_specs=(pl.BlockSpec(memory_space=pltpu.VMEM),) * 5,
        scratch_shapes=[
            pltpu.VMEM((n, width, width), jnp.float32),
            pltpu.VMEM((n, width, width - 128), jnp.bfloat16),
            pltpu.VMEM((n, width, width - 128), jnp.bfloat16),
            pltpu.VMEM((near + 1, n, 128, 128), jnp.float32),
        ]
        + [pltpu.VMEM((64, 128), jnp.float32)] * (n // 2),
        compiler_params=pltpu.CompilerParams(vmem_limit_bytes=56 * 1024 * 1024),
        cost_estimate=pl.CostEstimate(flops=2_000_000_000, bytes_accessed=5_000_000, transcendentals=4_000_000),
        name="factor",
    )(owner, slot, coords_all, coords_own)


MESH = pl.DeviceIdType.MESH
SIDE = 4
ROUTES = (("x", "z", "y"), ("y", "x", "z"), ("z", "y", "x"))
CAP = 12


def coordinates(index):
    return {
        "z": index // (4 * SIDE * 2),
        "x": lax.rem(index // (2 * SIDE), SIDE),
        "c": lax.rem(index // SIDE, 2),
        "y": lax.rem(index, SIDE),
    }


def place():
    return coordinates(lax.axis_index("blk") * SIDE + lax.axis_index("nb"))


def device(at, **moved):
    to = {**at, **moved}
    return (to["z"] * (2 * SIDE) + to["x"] * 2 + to["c"], to["y"])


def ahead(at, axis, k):
    return lax.rem(at[axis] + (k + SIDE), SIDE)


def meet(partners):
    barrier = pltpu.get_barrier_semaphore()
    for partner in partners:
        pl.semaphore_signal(barrier, inc=1, device_id=partner, device_id_type=MESH)
    pl.semaphore_wait(barrier, len(partners))


class Sender:
    def __init__(self, at, send, recv):
        self.at, self.send, self.recv, self.made = at, send, recv, []

    def push(self, src, dst, **moved):
        n = len(self.made)
        copy = pltpu.make_async_remote_copy(
            src_ref=src, dst_ref=dst, send_sem=self.send.at[n], recv_sem=self.recv.at[n],
            device_id=device(self.at, **moved), device_id_type=MESH,
        )
        self.made.append(copy)
        return copy

    def start(self, src, dst, **moved):
        copy = self.push(src, dst, **moved)
        copy.start()
        return copy

    def finish(self):
        for copy in self.made:
            copy.wait_send()


def ring_start(sender, axis, own, piece):
    me = sender.at[axis]
    return [sender.start(own, piece(me), **{axis: ahead(sender.at, axis, k)}) for k in (1, -1)]


def ring_pass(sender, axis, steps, piece, halves):
    out = []
    for copy, k, half in zip(steps, (1, -1), halves):
        copy.wait_recv()
        came = half(piece(ahead(sender.at, axis, -k)))
        out.append(sender.start(came, came, **{axis: ahead(sender.at, axis, k)}))
    return out


def open_kernel(*refs):
    count = len(ROUTES)
    note_ref, latent_ref, notes_ref = refs[:3]
    dense = refs[3:3 + count]
    own_sem, send, recv = refs[3 + count:]
    at = place()
    rows = dense[0].shape[-2]
    sender = Sender(at, send, recv)
    owns = [latent_ref.at[:, r * rows:(r + 1) * rows, :] for r in range(count)]
    local = [pltpu.make_async_copy(note_ref, notes_ref.at[at["z"], at["x"], at["c"], at["y"]], own_sem.at[count])]
    local += [
        pltpu.make_async_copy(owns[r], dense[r].at[at[f], at[s]], own_sem.at[r])
        for r, (_, f, s) in enumerate(ROUTES)
    ]
    for copy in local:
        copy.start()
    meet([device(at, **{axis: ahead(at, axis, k)}) for axis in "xyz" for k in (1, -1)] + [device(at, c=1 - at["c"])])

    def note_y(i):
        return notes_ref.at[at["z"], at["x"], at["c"], i]

    def note_x(i):
        return notes_ref.at[at["z"], i, at["c"]]

    def note_z(i):
        return notes_ref.at[i, :, at["c"]]

    def halves(n, axis=0):
        def cut(lo):
            return lambda ref: ref.at[pl.ds(lo, n)]
        return cut(0), cut(n)

    whole = (lambda ref: ref, lambda ref: ref)
    ny = ring_start(sender, "y", note_ref, note_y)
    second = [
        ring_start(sender, s, owns[r], lambda i, r=r, f=f: dense[r].at[at[f], i]) for r, (_, f, s) in enumerate(ROUTES)
    ]
    for copy in ny:
        copy.wait_recv()
    far = sender.start(note_y(ahead(at, "y", -1)), note_y(ahead(at, "y", -1)), y=ahead(at, "y", 1))
    local[0].wait()
    far.wait_recv()
    nx = ring_start(sender, "x", note_x(at["x"]), note_x)
    seconds = [
        ring_pass(sender, s, second[r], lambda i, r=r, f=f: dense[r].at[at[f], i], halves(4))
        for r, (_, f, s) in enumerate(ROUTES)
    ]
    nx = ring_pass(sender, "x", nx, note_x, halves(2))
    for copy in nx:
        copy.wait_recv()
    nz = ring_start(sender, "z", note_z(at["z"]), note_z)
    firsts = []
    for r, (_, f, s) in enumerate(ROUTES):
        local[1 + r].wait()
        for copy in seconds[r]:
            copy.wait_recv()
        firsts.append(ring_start(sender, f, dense[r].at[at[f]], lambda i, r=r: dense[r].at[i]))
    nz = ring_pass(sender, "z", nz, note_z, halves(2))
    for copy in nz:
        copy.wait_recv()
    nc = sender.start(notes_ref.at[:, :, at["c"]], notes_ref.at[:, :, at["c"]], c=1 - at["c"])
    last = [
        ring_pass(sender, f, firsts[r], lambda i, r=r: dense[r].at[i], halves(2)) for r, (_, f, _) in enumerate(ROUTES)
    ]
    for group in last:
        for copy in group:
            copy.wait_recv()
    nc.wait_recv()
    sender.finish()


def opening(note, latent, collective_id):
    count = len(ROUTES)
    slots, fields, points = latent.shape
    dense = jax.ShapeDtypeStruct((SIDE, SIDE, slots, fields // count, points), latent.dtype)
    copies = 2 + 1 + 4 + 4 + 1 + count * 8
    notes, *dense = pl.pallas_call(
        open_kernel,
        out_shape=(jax.ShapeDtypeStruct((SIDE, SIDE, 2, SIDE) + note.shape, note.dtype),) + (dense,) * count,
        in_specs=[pl.BlockSpec(memory_space=pltpu.VMEM), pl.BlockSpec(memory_space=pl.ANY)],
        out_specs=(pl.BlockSpec(memory_space=pltpu.VMEM),) + (pl.BlockSpec(memory_space=pl.ANY),) * count,
        scratch_shapes=[
            pltpu.SemaphoreType.DMA((count + 1,)),
            pltpu.SemaphoreType.DMA((copies,)),
            pltpu.SemaphoreType.DMA((copies,)),
        ],
        compiler_params=pltpu.CompilerParams(collective_id=collective_id, has_side_effects=True),
        name="opening",
    )(note, latent)
    return notes.reshape((2 * SIDE ** 3,) + note.shape), dense


def everywhere_kernel(x_ref, out_ref, own_sem, send, recv):
    at = place()
    sender = Sender(at, send, recv)
    own = pltpu.make_async_copy(x_ref, out_ref.at[at["z"], at["x"], at["c"], at["y"]], own_sem)
    own.start()
    meet([device(at, **{axis: ahead(at, axis, k)}) for axis in "yxz" for k in (1, 2, 3)] + [device(at, c=1 - at["c"])])
    line = out_ref.at[at["z"], at["x"], at["c"], at["y"]]
    stages = [
        [sender.push(x_ref, line, y=ahead(at, "y", k)) for k in (1, 2, 3)],
        [sender.push(out_ref.at[at["z"], at["x"], at["c"]], out_ref.at[at["z"], at["x"], at["c"]], x=ahead(at, "x", k)) for k in (1, 2, 3)],
        [sender.push(out_ref.at[at["z"], :, at["c"]], out_ref.at[at["z"], :, at["c"]], z=ahead(at, "z", k)) for k in (1, 2, 3)],
        [sender.push(out_ref.at[:, :, at["c"]], out_ref.at[:, :, at["c"]], c=1 - at["c"])],
    ]
    for number, stage in enumerate(stages):
        if number == 1:
            own.wait()
        for copy in stage:
            copy.start()
        for copy in stage:
            copy.wait_recv()
    sender.finish()


def everywhere(x, collective_id):
    out = pl.pallas_call(
        everywhere_kernel,
        out_shape=jax.ShapeDtypeStruct((SIDE, SIDE, 2, SIDE) + x.shape, x.dtype),
        in_specs=[pl.BlockSpec(memory_space=pltpu.VMEM)],
        out_specs=pl.BlockSpec(memory_space=pltpu.VMEM),
        scratch_shapes=[
            pltpu.SemaphoreType.DMA(()),
            pltpu.SemaphoreType.DMA((10,)),
            pltpu.SemaphoreType.DMA((10,)),
        ],
        compiler_params=pltpu.CompilerParams(collective_id=collective_id, has_side_effects=True),
        name="everywhere",
    )(x)
    return out.reshape((2 * SIDE ** 3,) + x.shape)


def deal_kernel(*refs):
    count = len(ROUTES)
    data, got, relay = refs[:count], refs[count:2 * count], refs[2 * count:3 * count]
    own_sem, send, recv = refs[3 * count:]
    at = place()
    c = at["c"]
    half = CAP // 2
    sender = Sender(at, send, recv)
    local = []
    for r, (axis, _, _) in enumerate(ROUTES):
        here = (at[axis], c)
        local.append(pltpu.make_async_copy(data[r].at[here], got[r].at[here], own_sem.at[r]))
        local[-1].start()
    meet(
        [device(at, **{axis: ahead(at, axis, k), "c": cc}) for axis in "xyz" for k in (1, -1) for cc in (0, 1)]
        + [device(at, c=1 - c)]
    )
    relays, plain = [], []
    for r, (axis, _, _) in enumerate(ROUTES):
        far = ahead(at, axis, 2)
        relays.append([
            sender.start(
                data[r].at[far, :, pl.ds(i * half, half)], relay[r].at[i], **{axis: ahead(at, axis, k)}
            )
            for i, k in enumerate((1, -1))
        ])
    for r, (axis, _, _) in enumerate(ROUTES):
        for k in (1, -1):
            to = ahead(at, axis, k)
            for cc in (c, 1 - c):
                plain.append(sender.start(data[r].at[to, cc], got[r].at[at[axis], c], **{axis: to, "c": cc}))
        plain.append(sender.start(data[r].at[at[axis], 1 - c], got[r].at[at[axis], c], c=1 - c))
    for r, (axis, _, _) in enumerate(ROUTES):
        for i, k in enumerate((1, -1)):
            relays[r][i].wait_recv()
            origin = ahead(at, axis, -k)
            for cc in (c, 1 - c):
                plain.append(sender.start(
                    relay[r].at[i, cc], got[r].at[origin, c, pl.ds(i * half, half)],
                    **{axis: ahead(at, axis, k), "c": cc},
                ))
    for copy in plain:
        copy.wait_recv()
    sender.finish()
    for copy in local:
        copy.wait()


def deal(data, collective_id):
    count = len(ROUTES)
    shapes = [jax.ShapeDtypeStruct(a.shape, a.dtype) for a in data]
    copies = (2 + 5 + 4) * count
    rows = data[0].shape[-2]
    return pl.pallas_call(
        deal_kernel,
        out_shape=tuple(shapes),
        in_specs=[pl.BlockSpec(memory_space=pl.ANY)] * count,
        out_specs=(pl.BlockSpec(memory_space=pl.ANY),) * count,
        scratch_shapes=[pltpu.VMEM((2, 2, CAP // 2, rows, 128), jnp.float32)] * count
        + [
            pltpu.SemaphoreType.DMA((count,)),
            pltpu.SemaphoreType.DMA((copies,)),
            pltpu.SemaphoreType.DMA((copies,)),
        ],
        compiler_params=pltpu.CompilerParams(collective_id=collective_id, has_side_effects=True),
        name="deal",
    )(*data)


def pick_kernel(*refs):
    count = len(ROUTES)
    meta, dense, out = refs[:count], refs[count:2 * count], refs[2 * count:]
    g = pl.program_id(0)
    for r in range(count):
        def copy(i, carry, r=r):
            out[r][0, i] = dense[r][meta[r][g * 128 + i]]
            return carry

        lax.fori_loop(0, meta[r][g * 128 + CAP], copy, 0)


def pile_kernel(*refs):
    count = len(ROUTES)
    meta, got, dense = refs[:count], refs[count:2 * count], refs[2 * count:]
    g = pl.program_id(0)

    @pl.when(g == 0)
    def _():
        for d in dense:
            def clear(i, carry, d=d):
                d[pl.ds(8 * i, 8)] = jnp.zeros((8,) + d.shape[1:], jnp.float32)
                return carry

            lax.fori_loop(0, d.shape[0] // 8, clear, 0)

    for r in range(count):
        def add(i, carry, r=r):
            to = meta[r][g * 128 + i]
            dense[r][to] = dense[r][to] + got[r][0, i]
            return carry

        lax.fori_loop(0, meta[r][g * 128 + CAP], add, 0)


def sort_items(kernel, name, meta, arrays, from_dense, places):
    count = len(ROUTES)
    rows = arrays[0].shape[-2]
    slab = pl.BlockSpec((1, CAP, rows, 128), lambda g, *m: (g, 0, 0, 0))
    whole = pl.BlockSpec((places, rows, 128), lambda g, *m: (0, 0, 0))
    slabs = jax.ShapeDtypeStruct((2 * SIDE, CAP, rows, 128), jnp.float32)
    wholes = jax.ShapeDtypeStruct((places, rows, 128), jnp.float32)
    source = wholes if from_dense else slabs
    return pl.pallas_call(
        kernel,
        out_shape=(slabs if from_dense else wholes,) * count,
        grid_spec=pltpu.PrefetchScalarGridSpec(
            num_scalar_prefetch=count,
            grid=(2 * SIDE,),
            in_specs=[whole if from_dense else slab] * count,
            out_specs=(slab if from_dense else whole,) * count,
        ),
        compiler_params=pltpu.CompilerParams(vmem_limit_bytes=40 * 1024 * 1024),
        name=name,
    )(*meta, *[a.reshape(source.shape) for a in arrays])


def fold_kernel(*refs):
    count = len(ROUTES)
    dense, out, mine = refs[:count], refs[count], refs[count + 1:2 * count + 1]
    passing, direct, second = (refs[(2 + i) * count + 1:(3 + i) * count + 1] for i in range(3))
    own_sem, send, recv = refs[5 * count + 1:]
    at = place()
    sender = Sender(at, send, recv)
    ways = (1, -1)
    cut = (pl.ds(0, 2), pl.ds(2, 2))
    local = []
    for r, (_, f, _) in enumerate(ROUTES):
        local.append([pltpu.make_async_copy(dense[r].at[at[f]], mine[r].at[0], own_sem.at[r, 0])] + [
            pltpu.make_async_copy(dense[r].at[ahead(at, f, k), cut[i]], mine[r].at[1, cut[i]], own_sem.at[r, 1 + i])
            for i, k in enumerate(ways)
        ])
        for copy in local[r]:
            copy.start()
    meet(
        [device(at, **{axis: ahead(at, axis, k)}) for axis in "xyz" for k in (1, 2, 3)]
    )
    ones, straight, twos, threes = [], [], [], []
    for r, (_, f, _) in enumerate(ROUTES):
        ones.append([
            sender.start(dense[r].at[ahead(at, f, 2), cut[i]], passing[r].at[0, cut[i]], **{f: ahead(at, f, k)})
            for i, k in enumerate(ways)
        ])
    for r, (_, f, _) in enumerate(ROUTES):
        straight.append([
            sender.start(dense[r].at[ahead(at, f, k), cut[1 - i]], direct[r].at[cut[1 - i]], **{f: ahead(at, f, k)})
            for i, k in enumerate(ways)
        ])
    for r, (_, f, _) in enumerate(ROUTES):
        twos.append([])
        for i, k in enumerate(ways):
            ones[r][i].wait_recv()
            local[r][1 + i].wait()
            mine[r][1, cut[i]] = mine[r][1, cut[i]] + passing[r][0, cut[i]]
            twos[r].append(sender.start(mine[r].at[1, cut[i]], passing[r].at[1, cut[i]], **{f: ahead(at, f, k)}))
    rows = out.shape[-2] // count
    for r, (_, f, s) in enumerate(ROUTES):
        local[r][0].wait()
        for copy in straight[r] + twos[r]:
            copy.wait_recv()
        mine[r][0] = (mine[r][0] + direct[r][...]) + passing[r][1]
        threes.append([
            sender.start(mine[r].at[0, ahead(at, s, k)], second[r].at[k - 1], **{s: ahead(at, s, k)}) for k in (1, 2, 3)
        ])
    for r, (_, f, s) in enumerate(ROUTES):
        for copy in threes[r]:
            copy.wait_recv()
        out[:, r * rows:(r + 1) * rows, :] = (mine[r][0, at[s]] + second[r][0]) + (second[r][1] + second[r][2])
    sender.finish()


def fold(dense, slots, collective_id):
    count = len(ROUTES)
    rows = dense[0].shape[-2]
    dense = [d.reshape(SIDE, SIDE, slots, rows, 128) for d in dense]
    part = (SIDE, slots, rows, 128)
    copies = (2 + 2 + 2 + 3) * count
    return pl.pallas_call(
        fold_kernel,
        out_shape=jax.ShapeDtypeStruct((slots, count * rows, 128), jnp.float32),
        in_specs=[pl.BlockSpec(memory_space=pl.ANY)] * count,
        out_specs=pl.BlockSpec(memory_space=pltpu.VMEM),
        scratch_shapes=[pltpu.VMEM((2,) + part, jnp.float32)] * count
        + [pltpu.VMEM((2,) + part, jnp.float32)] * count
        + [pltpu.VMEM(part, jnp.float32)] * count
        + [pltpu.VMEM((SIDE - 1,) + part[1:], jnp.float32)] * count
        + [
            pltpu.SemaphoreType.DMA((count, 3)),
            pltpu.SemaphoreType.DMA((copies,)),
            pltpu.SemaphoreType.DMA((copies,)),
        ],
        compiler_params=pltpu.CompilerParams(
            collective_id=collective_id, has_side_effects=True, vmem_limit_bytes=40 * 1024 * 1024
        ),
        name="fold",
    )(*dense)


def apply_kernel(routes, near, *refs):
    pos = refs[:routes]
    refs = refs[routes:]
    v, refs = refs[:routes * near], refs[routes * near:]
    own_ref, gh_ref, gl_ref, lh_ref, ll_ref = refs[:5]
    outs, u_ref = refs[5:5 + routes], refs[5 + routes]
    keep, sem = refs[6 + routes:]
    b = pl.program_id(0)
    slot = lax.rem(b, 2)
    rows = outs[0].shape[1]

    def copies(b, slot):
        return [
            pltpu.make_async_copy(
                keep.at[slot, k, pl.ds(r * rows, rows)], outs[r].at[pos[r][b * near + k]], sem.at[slot, k, r]
            )
            for k in range(near)
            for r in range(routes)
        ]

    values = jnp.concatenate(
        [jnp.concatenate([v[k * routes + r][0] for r in range(routes)], axis=0) for k in range(near)], axis=1
    )
    low = (lh_ref[0], ll_ref[0])
    g = (gh_ref[0], gl_ref[0])
    rest = own_ref[0] - wide(split(values), g, NT)
    u = wide(split(wide(split(rest), low, NT)), low)
    u_ref[0] = u
    pulled = -wide(split(u), g)

    @pl.when(b >= 2)
    def _():
        for copy in copies(b - 2, slot):
            copy.wait()

    for k in range(near):
        keep[slot, k] = pulled[:, k * 128:(k + 1) * 128]
    for copy in copies(b, slot):
        copy.start()

    @pl.when(b == pl.num_programs(0) - 1)
    def _():
        for copy in copies(b - 1, 1 - slot):
            copy.wait()
        for copy in copies(b, slot):
            copy.wait()


def apply_blocks(positions, got, latent, gh, gl, lh, ll):
    n, fields, points = latent.shape
    routes = len(positions)
    near = gh.shape[-1] // points
    rows = fields // routes

    def v_spec(k, r):
        return pl.BlockSpec((1, rows, points), lambda b, *pos: (pos[r][b * near + k], 0, 0))

    def b_spec(*shape):
        return pl.BlockSpec((1,) + shape, lambda b, *at: (b, 0, 0))

    got = [a.reshape(-1, rows, points) for a in got]
    return pl.pallas_call(
        functools.partial(apply_kernel, routes, near),
        out_shape=tuple(jax.ShapeDtypeStruct(a.shape, jnp.float32) for a in got)
        + (jax.ShapeDtypeStruct(latent.shape, jnp.float32),),
        grid_spec=pltpu.PrefetchScalarGridSpec(
            num_scalar_prefetch=routes,
            grid=(n,),
            in_specs=[v_spec(k, r) for k in range(near) for r in range(routes)]
            + [b_spec(fields, points)]
            + [b_spec(points, near * points)] * 2
            + [b_spec(points, points)] * 2,
            out_specs=(pl.BlockSpec(memory_space=pl.ANY),) * routes + (b_spec(fields, points),),
            scratch_shapes=[
                pltpu.VMEM((2, near, fields, points), jnp.float32),
                pltpu.SemaphoreType.DMA((2, near, routes)),
            ],
        ),
        name="apply",
    )(*positions, *([got[r] for k in range(near) for r in range(routes)]), latent, gh, gl, lh, ll)


def probit_ratio(margin):
    density = jnp.exp(-0.5 * margin * margin - 0.5 * math.log(2.0 * math.pi))
    mass = 0.5 * lax.erfc(-margin / math.sqrt(2.0))
    return density / mass


def rank_of(keys):
    count = keys.shape[-1]
    earlier = lax.broadcasted_iota(jnp.int32, (count, count), 1) < lax.broadcasted_iota(
        jnp.int32, (count, count), 0
    )
    same = keys[..., None, :] == keys[..., :, None]
    return jnp.sum(jnp.where(same & earlier, 1, 0), axis=-1).astype(jnp.int32)


def tables(at, named, places, slots):
    out = []
    for sparse, one, two in ROUTES:
        group_of = []
        for a in range(SIDE):
            for c in range(2):
                blk, nb = device({**at, sparse: a, "c": c})
                group_of.append(blk * SIDE + nb)
        rows = jnp.stack(group_of)
        asked, slot = named[rows], places[rows]
        lies = coordinates(asked)
        mine = (lies[sparse] == at[sparse]) & (lies["c"] == at["c"])
        to = (lies[one] * SIDE + lies[two]) * slots + slot
        keys = jnp.where(mine, 1, 0)
        rank = jnp.where(mine, rank_of(keys), -1)
        lane = lax.broadcasted_iota(jnp.int32, (2 * SIDE, 128, 1), 1)
        meta = jnp.sum(jnp.where(rank[:, None, :] == lane, to[:, None, :], 0), axis=2)
        meta = jnp.where(lane[:, :, 0] == CAP, jnp.sum(keys, axis=1)[:, None], meta)
        out.append(meta.astype(jnp.int32).reshape(-1))
    return out


def body(latent, coords, labels, owner, slot):
    block_count, field_count, point_count = latent.shape
    near_count = owner.shape[1]
    items = block_count * near_count
    axes = ("blk", "nb")
    device_count = lax.axis_size("blk") * lax.axis_size("nb")
    routes = len(ROUTES)
    rows = field_count // routes
    length = 2 * SIDE * CAP
    at = place()
    wanted = owner.reshape(-1)
    places = slot.reshape(-1)
    lies = coordinates(wanted)
    positions, most = [], 0
    for sparse, _, _ in ROUTES:
        group = lies[sparse] * 2 + lies["c"]
        rank = rank_of(group)
        most = jnp.maximum(most, jnp.max(rank))
        positions.append(group * CAP + jnp.minimum(rank, CAP - 1))
    flag = jnp.where(most >= CAP, 1, 0)
    line = jnp.concatenate([wanted, places, flag[None], jnp.zeros((127 - 2 * items,), jnp.int32)])
    note = jnp.concatenate(
        [
            coords.reshape(2 * block_count, point_count),
            jnp.broadcast_to(line.astype(jnp.float32)[None], (8, point_count)),
        ]
    )
    notes, dense = opening(note, latent, 1)
    lines = notes[:, 2 * block_count, :].astype(jnp.int32)
    crowded = jnp.max(lines[:, 2 * items]) > 0
    meta = tables(at, lines[:, :items], lines[:, items:2 * items], block_count)
    order = lax.broadcasted_iota(jnp.int32, (items,), 0)
    positions = [jnp.where(crowded, order, p) for p in positions]

    def pad_items(near):
        return [
            jnp.pad(near[:, r * rows:(r + 1) * rows, :], ((0, length - items), (0, 0), (0, 0))).reshape(
                2 * SIDE, CAP, rows, point_count
            )
            for r in range(routes)
        ]

    capacity = max(2, 2 * items // device_count)

    def requests():
        position = wanted * capacity + rank_of(wanted)
        sent = jnp.full((device_count * capacity,), -1, jnp.int32).at[position].set(places)
        asked = lax.all_to_all(
            sent.reshape(device_count, capacity), axes, split_axis=0, concat_axis=0, tiled=True
        ).reshape(-1)
        return position, asked

    def exchange(x):
        return lax.all_to_all(
            x.reshape(device_count, capacity, field_count, point_count),
            axes, split_axis=0, concat_axis=0, tiled=True,
        ).reshape(device_count * capacity, field_count, point_count)

    def routed_fetch():
        slabs = sort_items(pick_kernel, "pick", meta, dense, True, SIDE * SIDE * block_count)
        return tuple(
            a.reshape(2 * SIDE, CAP, rows, point_count)
            for a in deal([s.reshape(SIDE, 2, CAP, rows, point_count) for s in slabs], 3)
        )

    def padded_fetch():
        position, asked = requests()
        return tuple(pad_items(exchange(latent[jnp.maximum(asked, 0)])[position]))

    got = lax.cond(crowded, padded_fetch, routed_fetch)
    gh, gl, lh, ll, qdiag = factor(owner, slot, notes, coords)
    *data, own_part = apply_blocks(positions, got, latent, gh, gl, lh, ll)

    def routed_return():
        back = deal([d.reshape(SIDE, 2, CAP, rows, point_count) for d in data], 5)
        sums = sort_items(pile_kernel, "pile", meta, back, False, SIDE * SIDE * block_count)
        return fold(sums, block_count, 4)

    def padded_return():
        position, asked = requests()
        near = jnp.concatenate([d[:items] for d in data], axis=1)
        outgoing = jnp.zeros((device_count * capacity, field_count, point_count), jnp.float32)
        returned = exchange(outgoing.at[position].set(near))
        returned = jnp.where((asked >= 0)[:, None, None], returned, 0.0)
        return jnp.zeros_like(latent).at[jnp.maximum(asked, 0)].add(returned)

    prior = own_part + lax.cond(crowded, padded_return, routed_return)
    sign = 2.0 * labels.astype(jnp.float32) - 1.0
    margin = sign * latent
    ratio = probit_ratio(margin)
    weight = ratio * (ratio + margin)
    delta = (sign * ratio - prior) / (weight + qdiag)
    partial = jnp.sum(delta * delta, axis=(0, 2))
    spread = jnp.sum(everywhere(jnp.pad(partial, (0, 128 - field_count))[None], 2), axis=(0, 1))[:field_count]
    step_rms = jnp.sqrt(spread / (block_count * point_count * device_count) + 1e-06)
    new_latent = latent + 0.5 * delta / step_rms[None, :, None]
    return (new_latent, step_rms)


def solution(mesh):
    both = ("blk", "nb")
    return jax.shard_map(
        body,
        mesh=mesh,
        in_specs=(P(both, None, None), P(both, None, None), P(both, None, None), P(both, None), P(both, None)),
        out_specs=(P(both, None, None), P()),
        check_vma=False,
    )
```

```python
import math
import functools
import jax
import jax.numpy as jnp
from jax import lax
from jax.experimental import pallas as pl
from jax.experimental.pallas import tpu as pltpu
from jax.sharding import PartitionSpec as P

nugget = 0.25
length_scale = 0.1
NN = (((1,), (0,)), ((), ()))
NT = (((1,), (1,)), ((), ()))
TN = (((0,), (0,)), ((), ()))


def split(x):
    high = x.astype(jnp.bfloat16)
    return high, (x - high.astype(jnp.float32)).astype(jnp.bfloat16)


def dot(a, b, dims):
    return lax.dot_general(a, b, dims, preferred_element_type=jnp.float32)


def wide(a, b, dims=NN):
    ca, cb = dims[0][0][0], dims[0][1][0]
    left = jnp.concatenate([a[0], a[1], a[0]], axis=ca)
    right = jnp.concatenate([b[0], b[0], b[1]], axis=cb)
    return dot(left, right, dims)


def small(a, b, dims=NN):
    return dot(a[0], b[0], dims) + (dot(a[0], b[1], dims) + dot(a[1], b[0], dims))


def eliminate(packs):
    lane = lax.broadcasted_iota(jnp.int32, (8, 128), 1)
    row = lax.broadcasted_iota(jnp.int32, (8, 128), 0)
    base = lane & 64
    inner = lane & 63

    def pick(x, at):
        return jnp.take_along_axis(x, at, axis=1)

    for top in range(8):
        def step(t, carry, top=top):
            sub = 2 * t
            p = 8 * top + sub
            at0 = base + p
            at1 = at0 + 1
            first, second = inner == p, inner == p + 1
            own = first | second
            r1 = [jnp.broadcast_to(pack[pl.ds(p, 1), :], (8, 128)) for pack in packs]
            r2 = [jnp.broadcast_to(pack[pl.ds(p + 1, 1), :], (8, 128)) for pack in packs]
            tiles = [[pack[8 * s:8 * s + 8, :] for s in range(top, 8)] for pack in packs]
            a = [pick(x, at0) for x in r1]
            c1 = [[pick(y, at0) for y in ys] for ys in tiles]
            b = [pick(x, at1) for x in r1]
            d = [pick(x, at1) for x in r2]
            c2 = [[pick(y, at1) for y in ys] for ys in tiles]
            for q, pack in enumerate(packs):
                det = a[q] * d[q] - b[q] * b[q]
                rdet = 1.0 / det
                e1 = jnp.where(first, 1.0, jnp.where(second, 0.0, r1[q]))
                e2 = jnp.where(first, 0.0, jnp.where(second, 1.0, r2[q]))
                new1 = (d[q] * e1 - b[q] * e2) * rdet
                new2 = (a[q] * e2 - b[q] * e1) * rdet
                ra = lax.rsqrt(a[q])
                done1 = e1 * ra
                done2 = new2 * (det * (ra * lax.rsqrt(det)))
                for i, y in enumerate(tiles[q]):
                    x = jnp.where(own, 0.0, y) - c1[q][i] * new1 - c2[q][i] * new2
                    if i == 0:
                        x = jnp.where(row > sub + 1, x, jnp.where(row == sub, done1, jnp.where(row == sub + 1, done2, y)))
                    pack[8 * (top + i):8 * (top + i) + 8, :] = x
            return carry

        lax.fori_loop(0, 4, step, 0)


def lower64(x):
    keep = lax.broadcasted_iota(jnp.int32, (64, 64), 0) >= lax.broadcasted_iota(jnp.int32, (64, 64), 1)
    return jnp.where(keep, x, 0.0)


def factor_kernel(owner_ref, slot_ref, coords_ref, own_ref, gh_ref, gl_ref, lh_ref, ll_ref, qd_ref, cov, wh, wl, linv, *packs):
    n = own_ref.shape[0]
    near = owner_ref.shape[1]
    nt = near + 1
    last = near * 128
    scale = math.sqrt(3.0) / length_scale

    def build(m, carry):
        pts = [
            [coords_ref[owner_ref[m, k], pl.ds(2 * slot_ref[m, k] + i, 1), :] * scale for i in range(2)]
            for k in range(near)
        ] + [[own_ref[m, i:i + 1] * scale for i in range(2)]]
        for i in range(nt):
            xc = jnp.broadcast_to(pts[i][0], (128, 128)).T
            yc = jnp.broadcast_to(pts[i][1], (128, 128)).T
            for j in range(i + 1):
                dx = xc - pts[j][0]
                dy = yc - pts[j][1]
                q = dx * dx + dy * dy
                s = q * lax.rsqrt(jnp.maximum(q, 1e-30))
                c = (1.0 + s) * jnp.exp(-s)
                if i == j:
                    diag = lax.broadcasted_iota(jnp.int32, (128, 128), 0) == lax.broadcasted_iota(
                        jnp.int32, (128, 128), 1
                    )
                    c = c + jnp.where(diag, nugget, 0.0)
                cov[m, i * 128:(i + 1) * 128, j * 128:(j + 1) * 128] = c
        return carry

    lax.fori_loop(0, n, build, 0)

    def terms(ref_h, ref_l, *at):
        return ref_h[at], ref_l[at]

    for j in range(nt):
        lo, hi = j * 128, (j + 1) * 128
        rows = slice(lo, hi)

        if j:
            def left(m, carry):
                a = (wh[m, lo:, :lo], wl[m, lo:, :lo])
                b = (wh[m, lo:hi, :lo], wl[m, lo:hi, :lo])
                cov[m, lo:, lo:hi] = cov[m, lo:, lo:hi] - wide(a, b, NT)
                return carry

            lax.fori_loop(0, n, left, 0)

        for m in range(n):
            packs[m // 2][:, (m % 2) * 64:(m % 2) * 64 + 64] = cov[m, lo:lo + 64, lo:lo + 64]
        eliminate(packs)
        for m in range(n):
            at = (m % 2) * 64
            top = split(lower64(packs[m // 2][:, at:at + 64]))
            w = split(small(split(cov[m, lo + 64:hi, lo:lo + 64]), top, NT))
            linv[j, m, 0:64, 0:64] = top[0].astype(jnp.float32) + top[1].astype(jnp.float32)
            linv[j, m, 0:64, 64:128] = jnp.zeros((64, 64), jnp.float32)
            linv[j, m, 64:128, 0:64] = small(w, top)
            linv[j, m, 64:128, 64:128] = cov[m, lo + 64:hi, lo + 64:hi] - small(w, w, NT)
        for m in range(n):
            packs[m // 2][:, (m % 2) * 64:(m % 2) * 64 + 64] = linv[j, m, 64:128, 64:128]
        eliminate(packs)
        for m in range(n):
            at = (m % 2) * 64
            low = lower64(packs[m // 2][:, at:at + 64])
            linv[j, m, 64:128, 64:128] = low
            linv[j, m, 64:128, 0:64] = -small(split(low), split(linv[j, m, 64:128, 0:64]))

        if j < near:
            def panel(m, carry):
                w = split(wide(split(cov[m, hi:, lo:hi]), split(linv[j, m]), NT))
                wh[m, hi:, lo:hi] = w[0]
                wl[m, hi:, lo:hi] = w[1]
                return carry

            lax.fori_loop(0, n, panel, 0)

    def back(m, carry):
        for k in reversed(range(near)):
            lo, hi = k * 128, (k + 1) * 128
            g = wh[m, last:, lo:hi].astype(jnp.float32) + wl[m, last:, lo:hi].astype(jnp.float32)
            if hi < last:
                g = g - wide((gh_ref[m, :, hi:last], gl_ref[m, :, hi:last]), (wh[m, hi:last, lo:hi], wl[m, hi:last, lo:hi]))
            gh_ref[m, :, lo:hi], gl_ref[m, :, lo:hi] = split(wide(split(g), split(linv[k, m])))
        li = linv[near, m]
        lh_ref[m], ll_ref[m] = split(li)
        qd_ref[m] = jnp.sum(li * li, axis=0, keepdims=True)
        return carry

    lax.fori_loop(0, n, back, 0)


def factor(owner, slot, coords_all, coords_own):
    n, near = owner.shape
    width = (near + 1) * 128
    return pl.pallas_call(
        factor_kernel,
        out_shape=(jax.ShapeDtypeStruct((n, 128, near * 128), jnp.bfloat16),) * 2
        + (jax.ShapeDtypeStruct((n, 128, 128), jnp.bfloat16),) * 2
        + (jax.ShapeDtypeStruct((n, 1, 128), jnp.float32),),
        in_specs=[pl.BlockSpec(memory_space=pltpu.SMEM)] * 2 + [pl.BlockSpec(memory_space=pltpu.VMEM)] * 2,
        out_specs=(pl.BlockSpec(memory_space=pltpu.VMEM),) * 5,
        scratch_shapes=[
            pltpu.VMEM((n, width, width), jnp.float32),
            pltpu.VMEM((n, width, width - 128), jnp.bfloat16),
            pltpu.VMEM((n, width, width - 128), jnp.bfloat16),
            pltpu.VMEM((near + 1, n, 128, 128), jnp.float32),
        ]
        + [pltpu.VMEM((64, 128), jnp.float32)] * (n // 2),
        compiler_params=pltpu.CompilerParams(vmem_limit_bytes=56 * 1024 * 1024),
        cost_estimate=pl.CostEstimate(flops=2_000_000_000, bytes_accessed=5_000_000, transcendentals=4_000_000),
        name="factor",
    )(owner, slot, coords_all, coords_own)


MESH = pl.DeviceIdType.MESH
SIDE = 4
ROUTES = (("x", "z", "y"), ("y", "x", "z"), ("z", "y", "x"))
CAP = 12


def coordinates(index):
    return {
        "z": index // (4 * SIDE * 2),
        "x": lax.rem(index // (2 * SIDE), SIDE),
        "c": lax.rem(index // SIDE, 2),
        "y": lax.rem(index, SIDE),
    }


def place():
    return coordinates(lax.axis_index("blk") * SIDE + lax.axis_index("nb"))


def device(at, **moved):
    to = {**at, **moved}
    return (to["z"] * (2 * SIDE) + to["x"] * 2 + to["c"], to["y"])


def ahead(at, axis, k):
    return lax.rem(at[axis] + (k + SIDE), SIDE)


def meet(partners):
    barrier = pltpu.get_barrier_semaphore()
    for partner in partners:
        pl.semaphore_signal(barrier, inc=1, device_id=partner, device_id_type=MESH)
    pl.semaphore_wait(barrier, len(partners))


class Sender:
    def __init__(self, at, send, recv):
        self.at, self.send, self.recv, self.made = at, send, recv, []

    def push(self, src, dst, **moved):
        n = len(self.made)
        copy = pltpu.make_async_remote_copy(
            src_ref=src, dst_ref=dst, send_sem=self.send.at[n], recv_sem=self.recv.at[n],
            device_id=device(self.at, **moved), device_id_type=MESH,
        )
        self.made.append(copy)
        return copy

    def start(self, src, dst, **moved):
        copy = self.push(src, dst, **moved)
        copy.start()
        return copy

    def finish(self):
        for copy in self.made:
            copy.wait_send()


def everywhere_kernel(x_ref, out_ref, own_sem, send, recv):
    at = place()
    sender = Sender(at, send, recv)
    own = pltpu.make_async_copy(x_ref, out_ref.at[at["z"], at["x"], at["c"], at["y"]], own_sem)
    own.start()
    meet([device(at, **{axis: ahead(at, axis, k)}) for axis in "yxz" for k in (1, 2, 3)] + [device(at, c=1 - at["c"])])
    line = out_ref.at[at["z"], at["x"], at["c"], at["y"]]
    stages = [
        [sender.push(x_ref, line, y=ahead(at, "y", k)) for k in (1, 2, 3)],
        [sender.push(out_ref.at[at["z"], at["x"], at["c"]], out_ref.at[at["z"], at["x"], at["c"]], x=ahead(at, "x", k)) for k in (1, 2, 3)],
        [sender.push(out_ref.at[at["z"], :, at["c"]], out_ref.at[at["z"], :, at["c"]], z=ahead(at, "z", k)) for k in (1, 2, 3)],
        [sender.push(out_ref.at[:, :, at["c"]], out_ref.at[:, :, at["c"]], c=1 - at["c"])],
    ]
    for number, stage in enumerate(stages):
        if number == 1:
            own.wait()
        for copy in stage:
            copy.start()
        for copy in stage:
            copy.wait_recv()
    sender.finish()


def everywhere(x, collective_id):
    out = pl.pallas_call(
        everywhere_kernel,
        out_shape=jax.ShapeDtypeStruct((SIDE, SIDE, 2, SIDE) + x.shape, x.dtype),
        in_specs=[pl.BlockSpec(memory_space=pltpu.VMEM)],
        out_specs=pl.BlockSpec(memory_space=pltpu.VMEM),
        scratch_shapes=[
            pltpu.SemaphoreType.DMA(()),
            pltpu.SemaphoreType.DMA((10,)),
            pltpu.SemaphoreType.DMA((10,)),
        ],
        compiler_params=pltpu.CompilerParams(collective_id=collective_id, has_side_effects=True),
        name="everywhere",
    )(x)
    return out.reshape((2 * SIDE ** 3,) + x.shape)


def deal_kernel(*refs):
    count = len(ROUTES)
    data, got, relay = refs[:count], refs[count:2 * count], refs[2 * count:3 * count]
    own_sem, send, recv = refs[3 * count:]
    at = place()
    c = at["c"]
    half = CAP // 2
    sender = Sender(at, send, recv)
    local = []
    for r, (axis, _, _) in enumerate(ROUTES):
        here = (at[axis], c)
        local.append(pltpu.make_async_copy(data[r].at[here], got[r].at[here], own_sem.at[r]))
        local[-1].start()
    meet(
        [device(at, **{axis: ahead(at, axis, k), "c": cc}) for axis in "xyz" for k in (1, -1) for cc in (0, 1)]
        + [device(at, c=1 - c)]
    )
    relays, plain = [], []
    for r, (axis, _, _) in enumerate(ROUTES):
        far = ahead(at, axis, 2)
        relays.append([
            sender.start(
                data[r].at[far, :, pl.ds(i * half, half)], relay[r].at[i], **{axis: ahead(at, axis, k)}
            )
            for i, k in enumerate((1, -1))
        ])
    for r, (axis, _, _) in enumerate(ROUTES):
        for k in (1, -1):
            to = ahead(at, axis, k)
            for cc in (c, 1 - c):
                plain.append(sender.start(data[r].at[to, cc], got[r].at[at[axis], c], **{axis: to, "c": cc}))
        plain.append(sender.start(data[r].at[at[axis], 1 - c], got[r].at[at[axis], c], c=1 - c))
    for r, (axis, _, _) in enumerate(ROUTES):
        for i, k in enumerate((1, -1)):
            relays[r][i].wait_recv()
            origin = ahead(at, axis, -k)
            for cc in (c, 1 - c):
                plain.append(sender.start(
                    relay[r].at[i, cc], got[r].at[origin, c, pl.ds(i * half, half)],
                    **{axis: ahead(at, axis, k), "c": cc},
                ))
    for copy in plain:
        copy.wait_recv()
    sender.finish()
    for copy in local:
        copy.wait()


def deal(data, collective_id):
    count = len(ROUTES)
    shapes = [jax.ShapeDtypeStruct(a.shape, a.dtype) for a in data]
    copies = (2 + 5 + 4) * count
    rows = data[0].shape[-2]
    return pl.pallas_call(
        deal_kernel,
        out_shape=tuple(shapes),
        in_specs=[pl.BlockSpec(memory_space=pl.ANY)] * count,
        out_specs=(pl.BlockSpec(memory_space=pl.ANY),) * count,
        scratch_shapes=[pltpu.VMEM((2, 2, CAP // 2, rows, 128), jnp.float32)] * count
        + [
            pltpu.SemaphoreType.DMA((count,)),
            pltpu.SemaphoreType.DMA((copies,)),
            pltpu.SemaphoreType.DMA((copies,)),
        ],
        compiler_params=pltpu.CompilerParams(collective_id=collective_id, has_side_effects=True),
        name="deal",
    )(*data)


def pile_kernel(*refs):
    count = len(ROUTES)
    meta, got, dense = refs[0], refs[1:1 + count], refs[1 + count:]
    g = pl.program_id(0)

    @pl.when(g == 0)
    def _():
        for d in dense:
            def clear(i, carry, d=d):
                d[pl.ds(8 * i, 8)] = jnp.zeros((8,) + d.shape[1:], jnp.float32)
                return carry

            lax.fori_loop(0, d.shape[0] // 8, clear, 0)

    for r in range(count):
        def add(i, carry, r=r):
            to = meta[(r * 2 * SIDE + g) * 128 + i]
            dense[r][to] = dense[r][to] + got[r][0, i]
            return carry

        lax.fori_loop(0, meta[(r * 2 * SIDE + g) * 128 + CAP], add, 0)


def pile(meta, got, places):
    count = len(ROUTES)
    rows = got[0].shape[-2]
    slab = pl.BlockSpec((1, CAP, rows, 128), lambda g, *m: (g, 0, 0, 0))
    whole = pl.BlockSpec((places, rows, 128), lambda g, *m: (0, 0, 0))
    return pl.pallas_call(
        pile_kernel,
        out_shape=(jax.ShapeDtypeStruct((places, rows, 128), jnp.float32),) * count,
        grid_spec=pltpu.PrefetchScalarGridSpec(
            num_scalar_prefetch=1,
            grid=(2 * SIDE,),
            in_specs=[slab] * count,
            out_specs=(whole,) * count,
        ),
        compiler_params=pltpu.CompilerParams(vmem_limit_bytes=40 * 1024 * 1024),
        name="pile",
    )(meta, *[a.reshape(2 * SIDE, CAP, rows, 128) for a in got])


def fold_kernel(*refs):
    count = len(ROUTES)
    dense, out, mine = refs[:count], refs[count], refs[count + 1:2 * count + 1]
    passing, direct, second = (refs[(2 + i) * count + 1:(3 + i) * count + 1] for i in range(3))
    own_sem, send, recv = refs[5 * count + 1:]
    at = place()
    sender = Sender(at, send, recv)
    ways = (1, -1)
    cut = (pl.ds(0, 2), pl.ds(2, 2))
    local = []
    for r, (_, f, _) in enumerate(ROUTES):
        local.append([pltpu.make_async_copy(dense[r].at[at[f]], mine[r].at[0], own_sem.at[r, 0])] + [
            pltpu.make_async_copy(dense[r].at[ahead(at, f, k), cut[i]], mine[r].at[1, cut[i]], own_sem.at[r, 1 + i])
            for i, k in enumerate(ways)
        ])
        for copy in local[r]:
            copy.start()
    meet(
        [device(at, **{axis: ahead(at, axis, k)}) for axis in "xyz" for k in (1, 2, 3)]
    )
    ones, straight, twos, threes = [], [], [], []
    for r, (_, f, _) in enumerate(ROUTES):
        ones.append([
            sender.start(dense[r].at[ahead(at, f, 2), cut[i]], passing[r].at[0, cut[i]], **{f: ahead(at, f, k)})
            for i, k in enumerate(ways)
        ])
    for r, (_, f, _) in enumerate(ROUTES):
        straight.append([
            sender.start(dense[r].at[ahead(at, f, k), cut[1 - i]], direct[r].at[cut[1 - i]], **{f: ahead(at, f, k)})
            for i, k in enumerate(ways)
        ])
    for r, (_, f, _) in enumerate(ROUTES):
        twos.append([])
        for i, k in enumerate(ways):
            ones[r][i].wait_recv()
            local[r][1 + i].wait()
            mine[r][1, cut[i]] = mine[r][1, cut[i]] + passing[r][0, cut[i]]
            twos[r].append(sender.start(mine[r].at[1, cut[i]], passing[r].at[1, cut[i]], **{f: ahead(at, f, k)}))
    rows = out.shape[-2] // count
    for r, (_, f, s) in enumerate(ROUTES):
        local[r][0].wait()
        for copy in straight[r] + twos[r]:
            copy.wait_recv()
        mine[r][0] = (mine[r][0] + direct[r][...]) + passing[r][1]
        threes.append([
            sender.start(mine[r].at[0, ahead(at, s, k)], second[r].at[k - 1], **{s: ahead(at, s, k)}) for k in (1, 2, 3)
        ])
    for r, (_, f, s) in enumerate(ROUTES):
        for copy in threes[r]:
            copy.wait_recv()
        out[:, r * rows:(r + 1) * rows, :] = (mine[r][0, at[s]] + second[r][0]) + (second[r][1] + second[r][2])
    sender.finish()


def fold(dense, slots, collective_id):
    count = len(ROUTES)
    rows = dense[0].shape[-2]
    dense = [d.reshape(SIDE, SIDE, slots, rows, 128) for d in dense]
    part = (SIDE, slots, rows, 128)
    copies = (2 + 2 + 2 + 3) * count
    return pl.pallas_call(
        fold_kernel,
        out_shape=jax.ShapeDtypeStruct((slots, count * rows, 128), jnp.float32),
        in_specs=[pl.BlockSpec(memory_space=pl.ANY)] * count,
        out_specs=pl.BlockSpec(memory_space=pltpu.VMEM),
        scratch_shapes=[pltpu.VMEM((2,) + part, jnp.float32)] * count
        + [pltpu.VMEM((2,) + part, jnp.float32)] * count
        + [pltpu.VMEM(part, jnp.float32)] * count
        + [pltpu.VMEM((SIDE - 1,) + part[1:], jnp.float32)] * count
        + [
            pltpu.SemaphoreType.DMA((count, 3)),
            pltpu.SemaphoreType.DMA((copies,)),
            pltpu.SemaphoreType.DMA((copies,)),
        ],
        compiler_params=pltpu.CompilerParams(
            collective_id=collective_id, has_side_effects=True, vmem_limit_bytes=40 * 1024 * 1024
        ),
        name="fold",
    )(*dense)


def apply_kernel(routes, near, *refs):
    pos = refs[1]
    v, refs = refs[2:2 + near], refs[2 + near:]
    own_ref, gh_ref, gl_ref, lh_ref, ll_ref = refs[:5]
    outs, u_ref = refs[5:5 + routes], refs[5 + routes]
    keep, sem = refs[6 + routes:]
    b = pl.program_id(0)
    n = pl.num_programs(0)
    slot = lax.rem(b, 2)
    rows = outs[0].shape[1]

    def copies(b, slot):
        return [
            pltpu.make_async_copy(
                keep.at[slot, k, pl.ds(r * rows, rows)],
                outs[r].at[pos[(r * n + b) * near + k]],
                sem.at[slot, k, r],
            )
            for k in range(near)
            for r in range(routes)
        ]

    values = jnp.concatenate([v[k][0] for k in range(near)], axis=1)
    low = (lh_ref[0], ll_ref[0])
    g = (gh_ref[0], gl_ref[0])
    rest = own_ref[0] - wide(split(values), g, NT)
    u = wide(split(wide(split(rest), low, NT)), low)
    u_ref[0] = u
    pulled = -wide(split(u), g)

    @pl.when(b >= 2)
    def _():
        for copy in copies(b - 2, slot):
            copy.wait()

    for k in range(near):
        keep[slot, k] = pulled[:, k * 128:(k + 1) * 128]
    for copy in copies(b, slot):
        copy.start()

    @pl.when(b == n - 1)
    def _():
        for copy in copies(b - 1, 1 - slot):
            copy.wait()
        for copy in copies(b, slot):
            copy.wait()


def apply_blocks(nbr, positions, length, latent_all, latent, gh, gl, lh, ll):
    n, fields, points = latent.shape
    routes = len(ROUTES)
    near = nbr.shape[1]
    rows = fields // routes

    def v_spec(k):
        return pl.BlockSpec((1, fields, points), lambda b, nbr, pos: (nbr[b * near + k], 0, 0))

    def b_spec(*shape):
        return pl.BlockSpec((1,) + shape, lambda b, nbr, pos: (b, 0, 0))

    return pl.pallas_call(
        functools.partial(apply_kernel, routes, near),
        out_shape=(jax.ShapeDtypeStruct((length, rows, points), jnp.float32),) * routes
        + (jax.ShapeDtypeStruct(latent.shape, jnp.float32),),
        grid_spec=pltpu.PrefetchScalarGridSpec(
            num_scalar_prefetch=2,
            grid=(n,),
            in_specs=[v_spec(k) for k in range(near)]
            + [b_spec(fields, points)]
            + [b_spec(points, near * points)] * 2
            + [b_spec(points, points)] * 2,
            out_specs=(pl.BlockSpec(memory_space=pl.ANY),) * routes + (b_spec(fields, points),),
            scratch_shapes=[
                pltpu.VMEM((2, near, fields, points), jnp.float32),
                pltpu.SemaphoreType.DMA((2, near, routes)),
            ],
        ),
        name="apply",
    )(nbr.reshape(-1), positions, *([latent_all] * near), latent, gh, gl, lh, ll)


def probit_ratio(margin):
    density = jnp.exp(-0.5 * margin * margin - 0.5 * math.log(2.0 * math.pi))
    mass = 0.5 * lax.erfc(-margin / math.sqrt(2.0))
    return density / mass


def rank_of(keys):
    count = keys.shape[-1]
    earlier = lax.broadcasted_iota(jnp.int32, (count, count), 1) < lax.broadcasted_iota(
        jnp.int32, (count, count), 0
    )
    same = keys[..., None, :] == keys[..., :, None]
    return jnp.sum(jnp.where(same & earlier, 1, 0), axis=-1).astype(jnp.int32)


def tables(at, named, places, slots):
    out = []
    for sparse, one, two in ROUTES:
        group_of = []
        for a in range(SIDE):
            for c in range(2):
                blk, nb = device({**at, sparse: a, "c": c})
                group_of.append(blk * SIDE + nb)
        rows = jnp.stack(group_of)
        asked, slot = named[rows], places[rows]
        lies = coordinates(asked)
        mine = (lies[sparse] == at[sparse]) & (lies["c"] == at["c"])
        to = (lies[one] * SIDE + lies[two]) * slots + slot
        keys = jnp.where(mine, 1, 0)
        rank = jnp.where(mine, rank_of(keys), -1)
        lane = lax.broadcasted_iota(jnp.int32, (2 * SIDE, 128, 1), 1)
        meta = jnp.sum(jnp.where(rank[:, None, :] == lane, to[:, None, :], 0), axis=2)
        meta = jnp.where(lane[:, :, 0] == CAP, jnp.sum(keys, axis=1)[:, None], meta)
        out.append(meta.astype(jnp.int32).reshape(-1))
    return jnp.concatenate(out)


def body(latent, coords, labels, owner, slot):
    block_count, field_count, point_count = latent.shape
    near_count = owner.shape[1]
    items = block_count * near_count
    axes = ("blk", "nb")
    device_count = lax.axis_size("blk") * lax.axis_size("nb")
    routes = len(ROUTES)
    rows = field_count // routes
    length = 2 * SIDE * CAP
    at = place()
    wanted = owner.reshape(-1)
    places = slot.reshape(-1)
    lies = coordinates(wanted)
    positions, most = [], 0
    for sparse, _, _ in ROUTES:
        group = lies[sparse] * 2 + lies["c"]
        rank = rank_of(group)
        most = jnp.maximum(most, jnp.max(rank))
        positions.append(group * CAP + jnp.minimum(rank, CAP - 1))
    flag = jnp.where(most >= CAP, 1, 0)
    line = jnp.concatenate([wanted, places, flag[None], jnp.zeros((127 - 2 * items,), jnp.int32)])
    note = jnp.concatenate(
        [
            coords.reshape(2 * block_count, point_count),
            jnp.broadcast_to(line.astype(jnp.float32)[None], (8, point_count)),
        ]
    )
    notes = everywhere(note, 1)
    latent_all = lax.all_gather(latent, axes, axis=0, tiled=True)
    lines = notes[:, 2 * block_count, :].astype(jnp.int32)
    crowded = jnp.max(lines[:, 2 * items]) > 0
    meta = tables(at, lines[:, :items], lines[:, items:2 * items], block_count)
    order = lax.broadcasted_iota(jnp.int32, (items,), 0)
    positions = jnp.concatenate([jnp.where(crowded, order, p) for p in positions])
    capacity = max(2, 2 * items // device_count)

    def requests():
        position = wanted * capacity + rank_of(wanted)
        sent = jnp.full((device_count * capacity,), -1, jnp.int32).at[position].set(places)
        asked = lax.all_to_all(
            sent.reshape(device_count, capacity), axes, split_axis=0, concat_axis=0, tiled=True
        ).reshape(-1)
        return position, asked

    def exchange(x):
        return lax.all_to_all(
            x.reshape(device_count, capacity, field_count, point_count),
            axes, split_axis=0, concat_axis=0, tiled=True,
        ).reshape(device_count * capacity, field_count, point_count)

    gh, gl, lh, ll, qdiag = factor(owner, slot, notes, coords)
    *data, own_part = apply_blocks(
        owner * block_count + slot, positions, length, latent_all, latent, gh, gl, lh, ll
    )

    def routed_return():
        back = deal([d.reshape(SIDE, 2, CAP, rows, point_count) for d in data], 5)
        sums = pile(meta, back, SIDE * SIDE * block_count)
        return fold(sums, block_count, 4)

    def padded_return():
        position, asked = requests()
        near = jnp.concatenate([d[:items] for d in data], axis=1)
        outgoing = jnp.zeros((device_count * capacity, field_count, point_count), jnp.float32)
        returned = exchange(outgoing.at[position].set(near))
        returned = jnp.where((asked >= 0)[:, None, None], returned, 0.0)
        return jnp.zeros_like(latent).at[jnp.maximum(asked, 0)].add(returned)

    prior = own_part + lax.cond(crowded, padded_return, routed_return)
    sign = 2.0 * labels.astype(jnp.float32) - 1.0
    margin = sign * latent
    ratio = probit_ratio(margin)
    weight = ratio * (ratio + margin)
    delta = (sign * ratio - prior) / (weight + qdiag)
    partial = jnp.sum(delta * delta, axis=(0, 2))
    spread = jnp.sum(everywhere(jnp.pad(partial, (0, 128 - field_count))[None], 2), axis=(0, 1))[:field_count]
    step_rms = jnp.sqrt(spread / (block_count * point_count * device_count) + 1e-06)
    new_latent = latent + 0.5 * delta / step_rms[None, :, None]
    return (new_latent, step_rms)


def solution(mesh):
    both = ("blk", "nb")
    return jax.shard_map(
        body,
        mesh=mesh,
        in_specs=(P(both, None, None), P(both, None, None), P(both, None, None), P(both, None), P(both, None)),
        out_specs=(P(both, None, None), P()),
        check_vma=False,
    )
```

```python
import math
import functools
import jax
import jax.numpy as jnp
from jax import lax
from jax.experimental import pallas as pl
from jax.experimental.pallas import tpu as pltpu
from jax.sharding import PartitionSpec as P

nugget = 0.25
length_scale = 0.1
NN = (((1,), (0,)), ((), ()))
NT = (((1,), (1,)), ((), ()))
TN = (((0,), (0,)), ((), ()))


def split(x):
    high = x.astype(jnp.bfloat16)
    return high, (x - high.astype(jnp.float32)).astype(jnp.bfloat16)


def dot(a, b, dims):
    return lax.dot_general(a, b, dims, preferred_element_type=jnp.float32)


def wide(a, b, dims=NN):
    ca, cb = dims[0][0][0], dims[0][1][0]
    left = jnp.concatenate([a[0], a[1], a[0]], axis=ca)
    right = jnp.concatenate([b[0], b[0], b[1]], axis=cb)
    return dot(left, right, dims)


def small(a, b, dims=NN):
    return dot(a[0], b[0], dims) + (dot(a[0], b[1], dims) + dot(a[1], b[0], dims))


def eliminate(packs):
    lane = lax.broadcasted_iota(jnp.int32, (8, 128), 1)
    row = lax.broadcasted_iota(jnp.int32, (8, 128), 0)
    base = lane & 64
    inner = lane & 63

    def pick(x, at):
        return jnp.take_along_axis(x, at, axis=1)

    for top in range(8):
        def step(t, carry, top=top):
            sub = 2 * t
            p = 8 * top + sub
            at0 = base + p
            at1 = at0 + 1
            first, second = inner == p, inner == p + 1
            own = first | second
            r1 = [jnp.broadcast_to(pack[pl.ds(p, 1), :], (8, 128)) for pack in packs]
            r2 = [jnp.broadcast_to(pack[pl.ds(p + 1, 1), :], (8, 128)) for pack in packs]
            tiles = [[pack[8 * s:8 * s + 8, :] for s in range(top, 8)] for pack in packs]
            a = [pick(x, at0) for x in r1]
            c1 = [[pick(y, at0) for y in ys] for ys in tiles]
            b = [pick(x, at1) for x in r1]
            d = [pick(x, at1) for x in r2]
            c2 = [[pick(y, at1) for y in ys] for ys in tiles]
            for q, pack in enumerate(packs):
                det = a[q] * d[q] - b[q] * b[q]
                rdet = 1.0 / det
                e1 = jnp.where(first, 1.0, jnp.where(second, 0.0, r1[q]))
                e2 = jnp.where(first, 0.0, jnp.where(second, 1.0, r2[q]))
                new1 = (d[q] * e1 - b[q] * e2) * rdet
                new2 = (a[q] * e2 - b[q] * e1) * rdet
                ra = lax.rsqrt(a[q])
                done1 = e1 * ra
                done2 = new2 * (det * (ra * lax.rsqrt(det)))
                for i, y in enumerate(tiles[q]):
                    x = jnp.where(own, 0.0, y) - c1[q][i] * new1 - c2[q][i] * new2
                    if i == 0:
                        x = jnp.where(row > sub + 1, x, jnp.where(row == sub, done1, jnp.where(row == sub + 1, done2, y)))
                    pack[8 * (top + i):8 * (top + i) + 8, :] = x
            return carry

        lax.fori_loop(0, 4, step, 0)


def lower64(x):
    keep = lax.broadcasted_iota(jnp.int32, (64, 64), 0) >= lax.broadcasted_iota(jnp.int32, (64, 64), 1)
    return jnp.where(keep, x, 0.0)


def factor_kernel(owner_ref, slot_ref, coords_ref, own_ref, gh_ref, gl_ref, lh_ref, ll_ref, qd_ref, cov, wh, wl, linv, *packs):
    n = own_ref.shape[0]
    near = owner_ref.shape[1]
    nt = near + 1
    last = near * 128
    scale = math.sqrt(3.0) / length_scale

    def build(m, carry):
        pts = [
            [coords_ref[owner_ref[m, k], pl.ds(2 * slot_ref[m, k] + i, 1), :] * scale for i in range(2)]
            for k in range(near)
        ] + [[own_ref[m, i:i + 1] * scale for i in range(2)]]
        for i in range(nt):
            xc = jnp.broadcast_to(pts[i][0], (128, 128)).T
            yc = jnp.broadcast_to(pts[i][1], (128, 128)).T
            for j in range(i + 1):
                dx = xc - pts[j][0]
                dy = yc - pts[j][1]
                q = dx * dx + dy * dy
                s = q * lax.rsqrt(jnp.maximum(q, 1e-30))
                c = (1.0 + s) * jnp.exp(-s)
                if i == j:
                    diag = lax.broadcasted_iota(jnp.int32, (128, 128), 0) == lax.broadcasted_iota(
                        jnp.int32, (128, 128), 1
                    )
                    c = c + jnp.where(diag, nugget, 0.0)
                cov[m, i * 128:(i + 1) * 128, j * 128:(j + 1) * 128] = c
        return carry

    lax.fori_loop(0, n, build, 0)

    def terms(ref_h, ref_l, *at):
        return ref_h[at], ref_l[at]

    for j in range(nt):
        lo, hi = j * 128, (j + 1) * 128
        rows = slice(lo, hi)

        if j:
            def left(m, carry):
                a = (wh[m, lo:, :lo], wl[m, lo:, :lo])
                b = (wh[m, lo:hi, :lo], wl[m, lo:hi, :lo])
                cov[m, lo:, lo:hi] = cov[m, lo:, lo:hi] - wide(a, b, NT)
                return carry

            lax.fori_loop(0, n, left, 0)

        for m in range(n):
            packs[m // 2][:, (m % 2) * 64:(m % 2) * 64 + 64] = cov[m, lo:lo + 64, lo:lo + 64]
        eliminate(packs)
        for m in range(n):
            at = (m % 2) * 64
            top = split(lower64(packs[m // 2][:, at:at + 64]))
            w = split(small(split(cov[m, lo + 64:hi, lo:lo + 64]), top, NT))
            linv[j, m, 0:64, 0:64] = top[0].astype(jnp.float32) + top[1].astype(jnp.float32)
            linv[j, m, 0:64, 64:128] = jnp.zeros((64, 64), jnp.float32)
            linv[j, m, 64:128, 0:64] = small(w, top)
            linv[j, m, 64:128, 64:128] = cov[m, lo + 64:hi, lo + 64:hi] - small(w, w, NT)
        for m in range(n):
            packs[m // 2][:, (m % 2) * 64:(m % 2) * 64 + 64] = linv[j, m, 64:128, 64:128]
        eliminate(packs)
        for m in range(n):
            at = (m % 2) * 64
            low = lower64(packs[m // 2][:, at:at + 64])
            linv[j, m, 64:128, 64:128] = low
            linv[j, m, 64:128, 0:64] = -small(split(low), split(linv[j, m, 64:128, 0:64]))

        if j < near:
            def panel(m, carry):
                w = split(wide(split(cov[m, hi:, lo:hi]), split(linv[j, m]), NT))
                wh[m, hi:, lo:hi] = w[0]
                wl[m, hi:, lo:hi] = w[1]
                return carry

            lax.fori_loop(0, n, panel, 0)

    def back(m, carry):
        for k in reversed(range(near)):
            lo, hi = k * 128, (k + 1) * 128
            g = wh[m, last:, lo:hi].astype(jnp.float32) + wl[m, last:, lo:hi].astype(jnp.float32)
            if hi < last:
                g = g - wide((gh_ref[m, :, hi:last], gl_ref[m, :, hi:last]), (wh[m, hi:last, lo:hi], wl[m, hi:last, lo:hi]))
            gh_ref[m, :, lo:hi], gl_ref[m, :, lo:hi] = split(wide(split(g), split(linv[k, m])))
        li = linv[near, m]
        lh_ref[m], ll_ref[m] = split(li)
        qd_ref[m] = jnp.sum(li * li, axis=0, keepdims=True)
        return carry

    lax.fori_loop(0, n, back, 0)


def factor(owner, slot, coords_all, coords_own):
    n, near = owner.shape
    width = (near + 1) * 128
    return pl.pallas_call(
        factor_kernel,
        out_shape=(jax.ShapeDtypeStruct((n, 128, near * 128), jnp.bfloat16),) * 2
        + (jax.ShapeDtypeStruct((n, 128, 128), jnp.bfloat16),) * 2
        + (jax.ShapeDtypeStruct((n, 1, 128), jnp.float32),),
        in_specs=[pl.BlockSpec(memory_space=pltpu.SMEM)] * 2 + [pl.BlockSpec(memory_space=pltpu.VMEM)] * 2,
        out_specs=(pl.BlockSpec(memory_space=pltpu.VMEM),) * 5,
        scratch_shapes=[
            pltpu.VMEM((n, width, width), jnp.float32),
            pltpu.VMEM((n, width, width - 128), jnp.bfloat16),
            pltpu.VMEM((n, width, width - 128), jnp.bfloat16),
            pltpu.VMEM((near + 1, n, 128, 128), jnp.float32),
        ]
        + [pltpu.VMEM((64, 128), jnp.float32)] * (n // 2),
        compiler_params=pltpu.CompilerParams(vmem_limit_bytes=56 * 1024 * 1024),
        cost_estimate=pl.CostEstimate(flops=2_000_000_000, bytes_accessed=5_000_000, transcendentals=4_000_000),
        name="factor",
    )(owner, slot, coords_all, coords_own)


MESH = pl.DeviceIdType.MESH
SIDE = 4
ROUTES = (("x", "z", "y"), ("y", "x", "z"), ("z", "y", "x"))
CAP = 12


def coordinates(index):
    return {
        "z": index // (4 * SIDE * 2),
        "x": lax.rem(index // (2 * SIDE), SIDE),
        "c": lax.rem(index // SIDE, 2),
        "y": lax.rem(index, SIDE),
    }


def place():
    return coordinates(lax.axis_index("blk") * SIDE + lax.axis_index("nb"))


def device(at, **moved):
    to = {**at, **moved}
    return (to["z"] * (2 * SIDE) + to["x"] * 2 + to["c"], to["y"])


def ahead(at, axis, k):
    return lax.rem(at[axis] + (k + SIDE), SIDE)


def meet(partners):
    barrier = pltpu.get_barrier_semaphore()
    for partner in partners:
        pl.semaphore_signal(barrier, inc=1, device_id=partner, device_id_type=MESH)
    pl.semaphore_wait(barrier, len(partners))


class Sender:
    def __init__(self, at, send, recv):
        self.at, self.send, self.recv, self.made = at, send, recv, []

    def push(self, src, dst, **moved):
        n = len(self.made)
        copy = pltpu.make_async_remote_copy(
            src_ref=src, dst_ref=dst, send_sem=self.send.at[n], recv_sem=self.recv.at[n],
            device_id=device(self.at, **moved), device_id_type=MESH,
        )
        self.made.append(copy)
        return copy

    def start(self, src, dst, **moved):
        copy = self.push(src, dst, **moved)
        copy.start()
        return copy

    def finish(self):
        for copy in self.made:
            copy.wait_send()


def everywhere_kernel(x_ref, out_ref, own_sem, send, recv):
    at = place()
    sender = Sender(at, send, recv)
    own = pltpu.make_async_copy(x_ref, out_ref.at[at["z"], at["x"], at["c"], at["y"]], own_sem)
    own.start()
    meet([device(at, **{axis: ahead(at, axis, k)}) for axis in "yxz" for k in (1, 2, 3)] + [device(at, c=1 - at["c"])])
    line = out_ref.at[at["z"], at["x"], at["c"], at["y"]]
    stages = [
        [sender.push(x_ref, line, y=ahead(at, "y", k)) for k in (1, 2, 3)],
        [sender.push(out_ref.at[at["z"], at["x"], at["c"]], out_ref.at[at["z"], at["x"], at["c"]], x=ahead(at, "x", k)) for k in (1, 2, 3)],
        [sender.push(out_ref.at[at["z"], :, at["c"]], out_ref.at[at["z"], :, at["c"]], z=ahead(at, "z", k)) for k in (1, 2, 3)],
        [sender.push(out_ref.at[:, :, at["c"]], out_ref.at[:, :, at["c"]], c=1 - at["c"])],
    ]
    for number, stage in enumerate(stages):
        if number == 1:
            own.wait()
        for copy in stage:
            copy.start()
        for copy in stage:
            copy.wait_recv()
    sender.finish()


def everywhere(x, collective_id):
    out = pl.pallas_call(
        everywhere_kernel,
        out_shape=jax.ShapeDtypeStruct((SIDE, SIDE, 2, SIDE) + x.shape, x.dtype),
        in_specs=[pl.BlockSpec(memory_space=pltpu.VMEM)],
        out_specs=pl.BlockSpec(memory_space=pltpu.VMEM),
        scratch_shapes=[
            pltpu.SemaphoreType.DMA(()),
            pltpu.SemaphoreType.DMA((10,)),
            pltpu.SemaphoreType.DMA((10,)),
        ],
        compiler_params=pltpu.CompilerParams(collective_id=collective_id, has_side_effects=True),
        name="everywhere",
    )(x)
    return out.reshape((2 * SIDE ** 3,) + x.shape)


def deal_kernel(*refs):
    count = len(ROUTES)
    data, got, relay = refs[:count], refs[count:2 * count], refs[2 * count:3 * count]
    own_sem, send, recv = refs[3 * count:]
    at = place()
    c = at["c"]
    half = CAP // 2
    sender = Sender(at, send, recv)
    local = []
    for r, (axis, _, _) in enumerate(ROUTES):
        here = (at[axis], c)
        local.append(pltpu.make_async_copy(data[r].at[here], got[r].at[here], own_sem.at[r]))
        local[-1].start()
    meet(
        [device(at, **{axis: ahead(at, axis, k), "c": cc}) for axis in "xyz" for k in (1, -1) for cc in (0, 1)]
        + [device(at, c=1 - c)]
    )
    relays, plain = [], []
    for r, (axis, _, _) in enumerate(ROUTES):
        far = ahead(at, axis, 2)
        relays.append([
            sender.start(
                data[r].at[far, :, pl.ds(i * half, half)], relay[r].at[i], **{axis: ahead(at, axis, k)}
            )
            for i, k in enumerate((1, -1))
        ])
    for r, (axis, _, _) in enumerate(ROUTES):
        for k in (1, -1):
            to = ahead(at, axis, k)
            for cc in (c, 1 - c):
                plain.append(sender.start(data[r].at[to, cc], got[r].at[at[axis], c], **{axis: to, "c": cc}))
        plain.append(sender.start(data[r].at[at[axis], 1 - c], got[r].at[at[axis], c], c=1 - c))
    for r, (axis, _, _) in enumerate(ROUTES):
        for i, k in enumerate((1, -1)):
            relays[r][i].wait_recv()
            origin = ahead(at, axis, -k)
            for cc in (c, 1 - c):
                plain.append(sender.start(
                    relay[r].at[i, cc], got[r].at[origin, c, pl.ds(i * half, half)],
                    **{axis: ahead(at, axis, k), "c": cc},
                ))
    for copy in plain:
        copy.wait_recv()
    sender.finish()
    for copy in local:
        copy.wait()


def deal(data, collective_id):
    count = len(ROUTES)
    shapes = [jax.ShapeDtypeStruct(a.shape, a.dtype) for a in data]
    copies = (2 + 5 + 4) * count
    rows = data[0].shape[-2]
    return pl.pallas_call(
        deal_kernel,
        out_shape=tuple(shapes),
        in_specs=[pl.BlockSpec(memory_space=pl.ANY)] * count,
        out_specs=(pl.BlockSpec(memory_space=pl.ANY),) * count,
        scratch_shapes=[pltpu.VMEM((2, 2, CAP // 2, rows, 128), jnp.float32)] * count
        + [
            pltpu.SemaphoreType.DMA((count,)),
            pltpu.SemaphoreType.DMA((copies,)),
            pltpu.SemaphoreType.DMA((copies,)),
        ],
        compiler_params=pltpu.CompilerParams(collective_id=collective_id, has_side_effects=True),
        name="deal",
    )(*data)


def pile_kernel(*refs):
    count = len(ROUTES)
    meta, got, dense = refs[0], refs[1:1 + count], refs[1 + count:]
    g = pl.program_id(0)

    @pl.when(g == 0)
    def _():
        for d in dense:
            def clear(i, carry, d=d):
                d[pl.ds(8 * i, 8)] = jnp.zeros((8,) + d.shape[1:], jnp.float32)
                return carry

            lax.fori_loop(0, d.shape[0] // 8, clear, 0)

    for r in range(count):
        def add(i, carry, r=r):
            to = meta[(r * 2 * SIDE + g) * 128 + i]
            dense[r][to] = dense[r][to] + got[r][0, i]
            return carry

        lax.fori_loop(0, meta[(r * 2 * SIDE + g) * 128 + CAP], add, 0)


def pile(meta, got, places):
    count = len(ROUTES)
    rows = got[0].shape[-2]
    slab = pl.BlockSpec((1, CAP, rows, 128), lambda g, *m: (g, 0, 0, 0))
    whole = pl.BlockSpec((places, rows, 128), lambda g, *m: (0, 0, 0))
    return pl.pallas_call(
        pile_kernel,
        out_shape=(jax.ShapeDtypeStruct((places, rows, 128), jnp.float32),) * count,
        grid_spec=pltpu.PrefetchScalarGridSpec(
            num_scalar_prefetch=1,
            grid=(2 * SIDE,),
            in_specs=[slab] * count,
            out_specs=(whole,) * count,
        ),
        compiler_params=pltpu.CompilerParams(vmem_limit_bytes=40 * 1024 * 1024),
        name="pile",
    )(meta, *[a.reshape(2 * SIDE, CAP, rows, 128) for a in got])


def fold_kernel(scale, *refs):
    count = len(ROUTES)
    dense, (pull_ref, own_ref, weight_ref, latent_ref, new_ref, rms_ref) = refs[:count], refs[count:count + 6]
    refs = refs[count + 6:]
    mine, passing, direct, second = (refs[i * count:(i + 1) * count] for i in range(4))
    delta, line, total, own_sem, line_sem, send, recv = refs[4 * count:]
    at = place()
    sender = Sender(at, send, recv)
    ways = (1, -1)
    cut = (pl.ds(0, 2), pl.ds(2, 2))
    local = []
    for r, (_, f, _) in enumerate(ROUTES):
        local.append([pltpu.make_async_copy(dense[r].at[at[f]], mine[r].at[0], own_sem.at[r, 0])] + [
            pltpu.make_async_copy(dense[r].at[ahead(at, f, k), cut[i]], mine[r].at[1, cut[i]], own_sem.at[r, 1 + i])
            for i, k in enumerate(ways)
        ])
        for copy in local[r]:
            copy.start()
    meet(
        [device(at, **{axis: ahead(at, axis, k)}) for axis in "xyz" for k in (1, 2, 3)] + [device(at, c=1 - at["c"])]
    )
    ones, straight, twos, threes = [], [], [], []
    for r, (_, f, _) in enumerate(ROUTES):
        ones.append([
            sender.start(dense[r].at[ahead(at, f, 2), cut[i]], passing[r].at[0, cut[i]], **{f: ahead(at, f, k)})
            for i, k in enumerate(ways)
        ])
    for r, (_, f, _) in enumerate(ROUTES):
        straight.append([
            sender.start(dense[r].at[ahead(at, f, k), cut[1 - i]], direct[r].at[cut[1 - i]], **{f: ahead(at, f, k)})
            for i, k in enumerate(ways)
        ])
    for r, (_, f, _) in enumerate(ROUTES):
        twos.append([])
        for i, k in enumerate(ways):
            ones[r][i].wait_recv()
            local[r][1 + i].wait()
            mine[r][1, cut[i]] = mine[r][1, cut[i]] + passing[r][0, cut[i]]
            twos[r].append(sender.start(mine[r].at[1, cut[i]], passing[r].at[1, cut[i]], **{f: ahead(at, f, k)}))
    rows = new_ref.shape[-2] // count
    for r, (_, f, s) in enumerate(ROUTES):
        local[r][0].wait()
        for copy in straight[r] + twos[r]:
            copy.wait_recv()
        mine[r][0] = (mine[r][0] + direct[r][...]) + passing[r][1]
        threes.append([
            sender.start(mine[r].at[0, ahead(at, s, k)], second[r].at[k - 1], **{s: ahead(at, s, k)}) for k in (1, 2, 3)
        ])
    squares = []
    for r, (_, f, s) in enumerate(ROUTES):
        part = slice(r * rows, (r + 1) * rows)
        known = pull_ref[:, part, :] - own_ref[:, part, :]
        for copy in threes[r]:
            copy.wait_recv()
        prior = (mine[r][0, at[s]] + second[r][0]) + (second[r][1] + second[r][2])
        d = (known - prior) / weight_ref[:, part, :]
        delta[:, part, :] = d
        squares.append(jnp.sum(d * d, axis=0))
    squares.append(jnp.zeros((128 - rows * count, 128), jnp.float32))
    line[...] = jnp.sum(jnp.concatenate(squares, axis=0).T, axis=0, keepdims=True)
    here = total.at[at["z"], at["x"], at["c"], at["y"]]
    keep = pltpu.make_async_copy(line, here, line_sem)
    keep.start()
    keep.wait()
    plane, sheet, side = total.at[at["z"], at["x"], at["c"]], total.at[at["z"], :, at["c"]], total.at[:, :, at["c"]]
    for axis, src in (("y", here), ("x", plane), ("z", sheet)):
        stage = [sender.start(src, src, **{axis: ahead(at, axis, k)}) for k in (1, 2, 3)]
        for copy in stage:
            copy.wait_recv()
    sender.start(side, side, c=1 - at["c"]).wait_recv()
    spread = jnp.sum(total[...], axis=(0, 1, 2, 3))
    rms = jnp.sqrt(spread * scale + 1e-06)
    rms_ref[...] = rms
    step = jnp.broadcast_to(0.5 / rms, (128, 128)).T[:rows * count]
    for b in range(new_ref.shape[0]):
        new_ref[b] = latent_ref[b] + delta[b] * step
    sender.finish()


def fold(dense, pull, own_part, weight, latent, points, collective_id):
    count = len(ROUTES)
    slots = latent.shape[0]
    rows = dense[0].shape[-2]
    dense = [d.reshape(SIDE, SIDE, slots, rows, 128) for d in dense]
    part = (SIDE, slots, rows, 128)
    copies = (2 + 2 + 2 + 3) * count + 10
    return pl.pallas_call(
        functools.partial(fold_kernel, 1.0 / points),
        out_shape=(
            jax.ShapeDtypeStruct(latent.shape, jnp.float32),
            jax.ShapeDtypeStruct((1, 128), jnp.float32),
        ),
        in_specs=[pl.BlockSpec(memory_space=pl.ANY)] * count + [pl.BlockSpec(memory_space=pltpu.VMEM)] * 4,
        out_specs=(pl.BlockSpec(memory_space=pltpu.VMEM),) * 2,
        scratch_shapes=[pltpu.VMEM((2,) + part, jnp.float32)] * count
        + [pltpu.VMEM((2,) + part, jnp.float32)] * count
        + [pltpu.VMEM(part, jnp.float32)] * count
        + [pltpu.VMEM((SIDE - 1,) + part[1:], jnp.float32)] * count
        + [
            pltpu.VMEM(latent.shape, jnp.float32),
            pltpu.VMEM((1, 128), jnp.float32),
            pltpu.VMEM((SIDE, SIDE, 2, SIDE, 1, 128), jnp.float32),
            pltpu.SemaphoreType.DMA((count, 3)),
            pltpu.SemaphoreType.DMA(()),
            pltpu.SemaphoreType.DMA((copies,)),
            pltpu.SemaphoreType.DMA((copies,)),
        ],
        compiler_params=pltpu.CompilerParams(
            collective_id=collective_id, has_side_effects=True, vmem_limit_bytes=40 * 1024 * 1024
        ),
        name="fold",
    )(*dense, pull, own_part, weight, latent)


def apply_kernel(routes, near, *refs):
    pos = refs[1]
    v, refs = refs[2:2 + near], refs[2 + near:]
    own_ref, gh_ref, gl_ref, lh_ref, ll_ref = refs[:5]
    outs, u_ref = refs[5:5 + routes], refs[5 + routes]
    keep, sem = refs[6 + routes:]
    b = pl.program_id(0)
    n = pl.num_programs(0)
    slot = lax.rem(b, 2)
    rows = outs[0].shape[1]

    def copies(b, slot):
        return [
            pltpu.make_async_copy(
                keep.at[slot, k, pl.ds(r * rows, rows)],
                outs[r].at[pos[(r * n + b) * near + k]],
                sem.at[slot, k, r],
            )
            for k in range(near)
            for r in range(routes)
        ]

    values = jnp.concatenate([v[k][0] for k in range(near)], axis=1)
    low = (lh_ref[0], ll_ref[0])
    g = (gh_ref[0], gl_ref[0])
    rest = own_ref[0] - wide(split(values), g, NT)
    u = wide(split(wide(split(rest), low, NT)), low)
    u_ref[0] = u
    pulled = -wide(split(u), g)

    @pl.when(b >= 2)
    def _():
        for copy in copies(b - 2, slot):
            copy.wait()

    for k in range(near):
        keep[slot, k] = pulled[:, k * 128:(k + 1) * 128]
    for copy in copies(b, slot):
        copy.start()

    @pl.when(b == n - 1)
    def _():
        for copy in copies(b - 1, 1 - slot):
            copy.wait()
        for copy in copies(b, slot):
            copy.wait()


def apply_blocks(nbr, positions, length, latent_all, latent, gh, gl, lh, ll):
    n, fields, points = latent.shape
    routes = len(ROUTES)
    near = nbr.shape[1]
    rows = fields // routes

    def v_spec(k):
        return pl.BlockSpec((1, fields, points), lambda b, nbr, pos: (nbr[b * near + k], 0, 0))

    def b_spec(*shape):
        return pl.BlockSpec((1,) + shape, lambda b, nbr, pos: (b, 0, 0))

    return pl.pallas_call(
        functools.partial(apply_kernel, routes, near),
        out_shape=(jax.ShapeDtypeStruct((length, rows, points), jnp.float32),) * routes
        + (jax.ShapeDtypeStruct(latent.shape, jnp.float32),),
        grid_spec=pltpu.PrefetchScalarGridSpec(
            num_scalar_prefetch=2,
            grid=(n,),
            in_specs=[v_spec(k) for k in range(near)]
            + [b_spec(fields, points)]
            + [b_spec(points, near * points)] * 2
            + [b_spec(points, points)] * 2,
            out_specs=(pl.BlockSpec(memory_space=pl.ANY),) * routes + (b_spec(fields, points),),
            scratch_shapes=[
                pltpu.VMEM((2, near, fields, points), jnp.float32),
                pltpu.SemaphoreType.DMA((2, near, routes)),
            ],
        ),
        name="apply",
    )(nbr.reshape(-1), positions, *([latent_all] * near), latent, gh, gl, lh, ll)


def probit_ratio(margin):
    density = jnp.exp(-0.5 * margin * margin - 0.5 * math.log(2.0 * math.pi))
    mass = 0.5 * lax.erfc(-margin / math.sqrt(2.0))
    return density / mass


def rank_of(keys):
    count = keys.shape[-1]
    earlier = lax.broadcasted_iota(jnp.int32, (count, count), 1) < lax.broadcasted_iota(
        jnp.int32, (count, count), 0
    )
    same = keys[..., None, :] == keys[..., :, None]
    return jnp.sum(jnp.where(same & earlier, 1, 0), axis=-1).astype(jnp.int32)


def tables(at, named, places, slots):
    out = []
    for sparse, one, two in ROUTES:
        group_of = []
        for a in range(SIDE):
            for c in range(2):
                blk, nb = device({**at, sparse: a, "c": c})
                group_of.append(blk * SIDE + nb)
        rows = jnp.stack(group_of)
        asked, slot = named[rows], places[rows]
        lies = coordinates(asked)
        mine = (lies[sparse] == at[sparse]) & (lies["c"] == at["c"])
        to = (lies[one] * SIDE + lies[two]) * slots + slot
        keys = jnp.where(mine, 1, 0)
        rank = jnp.where(mine, rank_of(keys), -1)
        lane = lax.broadcasted_iota(jnp.int32, (2 * SIDE, 128, 1), 1)
        meta = jnp.sum(jnp.where(rank[:, None, :] == lane, to[:, None, :], 0), axis=2)
        meta = jnp.where(lane[:, :, 0] == CAP, jnp.sum(keys, axis=1)[:, None], meta)
        out.append(meta.astype(jnp.int32).reshape(-1))
    return jnp.concatenate(out)


def body(latent, coords, labels, owner, slot):
    block_count, field_count, point_count = latent.shape
    near_count = owner.shape[1]
    items = block_count * near_count
    axes = ("blk", "nb")
    device_count = lax.axis_size("blk") * lax.axis_size("nb")
    routes = len(ROUTES)
    rows = field_count // routes
    length = 2 * SIDE * CAP
    at = place()
    wanted = owner.reshape(-1)
    places = slot.reshape(-1)
    lies = coordinates(wanted)
    positions, most = [], 0
    for sparse, _, _ in ROUTES:
        group = lies[sparse] * 2 + lies["c"]
        rank = rank_of(group)
        most = jnp.maximum(most, jnp.max(rank))
        positions.append(group * CAP + jnp.minimum(rank, CAP - 1))
    flag = jnp.where(most >= CAP, 1, 0)
    line = jnp.concatenate([wanted, places, flag[None], jnp.zeros((127 - 2 * items,), jnp.int32)])
    note = jnp.concatenate(
        [
            coords.reshape(2 * block_count, point_count),
            jnp.broadcast_to(line.astype(jnp.float32)[None], (8, point_count)),
        ]
    )
    notes = everywhere(note, 1)
    latent_all = lax.all_gather(latent, axes, axis=0, tiled=True)
    lines = notes[:, 2 * block_count, :].astype(jnp.int32)
    crowded = jnp.max(lines[:, 2 * items]) > 0
    meta = tables(at, lines[:, :items], lines[:, items:2 * items], block_count)
    order = lax.broadcasted_iota(jnp.int32, (items,), 0)
    positions = jnp.concatenate([jnp.where(crowded, order, p) for p in positions])
    capacity = max(2, 2 * items // device_count)

    def requests():
        position = wanted * capacity + rank_of(wanted)
        sent = jnp.full((device_count * capacity,), -1, jnp.int32).at[position].set(places)
        asked = lax.all_to_all(
            sent.reshape(device_count, capacity), axes, split_axis=0, concat_axis=0, tiled=True
        ).reshape(-1)
        return position, asked

    def exchange(x):
        return lax.all_to_all(
            x.reshape(device_count, capacity, field_count, point_count),
            axes, split_axis=0, concat_axis=0, tiled=True,
        ).reshape(device_count * capacity, field_count, point_count)

    gh, gl, lh, ll, qdiag = factor(owner, slot, notes, coords)
    *data, own_part = apply_blocks(
        owner * block_count + slot, positions, length, latent_all, latent, gh, gl, lh, ll
    )

    sign = 2.0 * labels.astype(jnp.float32) - 1.0
    margin = sign * latent
    ratio = probit_ratio(margin)
    pull = sign * ratio
    weight = ratio * (ratio + margin) + qdiag
    point_total = block_count * point_count * device_count

    def routed_return():
        back = deal([d.reshape(SIDE, 2, CAP, rows, point_count) for d in data], 5)
        sums = pile(meta, back, SIDE * SIDE * block_count)
        new_latent, rms = fold(sums, pull, own_part, weight, latent, point_total, 4)
        return new_latent, rms[0, :field_count]

    def padded_return():
        position, asked = requests()
        near = jnp.concatenate([d[:items] for d in data], axis=1)
        outgoing = jnp.zeros((device_count * capacity, field_count, point_count), jnp.float32)
        returned = exchange(outgoing.at[position].set(near))
        returned = jnp.where((asked >= 0)[:, None, None], returned, 0.0)
        prior = own_part.at[jnp.maximum(asked, 0)].add(returned)
        delta = (pull - prior) / weight
        partial = jnp.sum(delta * delta, axis=(0, 2))
        spread = jnp.sum(everywhere(jnp.pad(partial, (0, 128 - field_count))[None], 2), axis=(0, 1))[:field_count]
        step_rms = jnp.sqrt(spread / point_total + 1e-06)
        return latent + 0.5 * delta / step_rms[None, :, None], step_rms

    return lax.cond(crowded, padded_return, routed_return)


def solution(mesh):
    both = ("blk", "nb")
    return jax.shard_map(
        body,
        mesh=mesh,
        in_specs=(P(both, None, None), P(both, None, None), P(both, None, None), P(both, None), P(both, None)),
        out_specs=(P(both, None, None), P()),
        check_vma=False,
    )
```

```python
import math
import functools
import jax
import jax.numpy as jnp
from jax import lax
from jax.experimental import pallas as pl
from jax.experimental.pallas import tpu as pltpu
from jax.sharding import PartitionSpec as P

nugget = 0.25
length_scale = 0.1
NN = (((1,), (0,)), ((), ()))
NT = (((1,), (1,)), ((), ()))
TN = (((0,), (0,)), ((), ()))


def split(x):
    high = x.astype(jnp.bfloat16)
    return high, (x - high.astype(jnp.float32)).astype(jnp.bfloat16)


def dot(a, b, dims):
    return lax.dot_general(a, b, dims, preferred_element_type=jnp.float32)


def wide(a, b, dims=NN):
    ca, cb = dims[0][0][0], dims[0][1][0]
    left = jnp.concatenate([a[0], a[1], a[0]], axis=ca)
    right = jnp.concatenate([b[0], b[0], b[1]], axis=cb)
    return dot(left, right, dims)


def small(a, b, dims=NN):
    return dot(a[0], b[0], dims) + (dot(a[0], b[1], dims) + dot(a[1], b[0], dims))


def eliminate(packs):
    lane = lax.broadcasted_iota(jnp.int32, (8, 128), 1)
    row = lax.broadcasted_iota(jnp.int32, (8, 128), 0)
    base = lane & 64
    inner = lane & 63

    def pick(x, at):
        return jnp.take_along_axis(x, at, axis=1)

    for top in range(8):
        def step(t, carry, top=top):
            sub = 2 * t
            p = 8 * top + sub
            at0 = base + p
            at1 = at0 + 1
            first, second = inner == p, inner == p + 1
            own = first | second
            r1 = [jnp.broadcast_to(pack[pl.ds(p, 1), :], (8, 128)) for pack in packs]
            r2 = [jnp.broadcast_to(pack[pl.ds(p + 1, 1), :], (8, 128)) for pack in packs]
            tiles = [[pack[8 * s:8 * s + 8, :] for s in range(top, 8)] for pack in packs]
            a = [pick(x, at0) for x in r1]
            c1 = [[pick(y, at0) for y in ys] for ys in tiles]
            b = [pick(x, at1) for x in r1]
            d = [pick(x, at1) for x in r2]
            c2 = [[pick(y, at1) for y in ys] for ys in tiles]
            for q, pack in enumerate(packs):
                det = a[q] * d[q] - b[q] * b[q]
                rdet = 1.0 / det
                e1 = jnp.where(first, 1.0, jnp.where(second, 0.0, r1[q]))
                e2 = jnp.where(first, 0.0, jnp.where(second, 1.0, r2[q]))
                new1 = (d[q] * e1 - b[q] * e2) * rdet
                new2 = (a[q] * e2 - b[q] * e1) * rdet
                ra = lax.rsqrt(a[q])
                done1 = e1 * ra
                done2 = new2 * (det * (ra * lax.rsqrt(det)))
                for i, y in enumerate(tiles[q]):
                    x = jnp.where(own, 0.0, y) - c1[q][i] * new1 - c2[q][i] * new2
                    if i == 0:
                        x = jnp.where(row > sub + 1, x, jnp.where(row == sub, done1, jnp.where(row == sub + 1, done2, y)))
                    pack[8 * (top + i):8 * (top + i) + 8, :] = x
            return carry

        lax.fori_loop(0, 4, step, 0)


def lower64(x):
    keep = lax.broadcasted_iota(jnp.int32, (64, 64), 0) >= lax.broadcasted_iota(jnp.int32, (64, 64), 1)
    return jnp.where(keep, x, 0.0)


def factor_kernel(owner_ref, slot_ref, coords_ref, own_ref, gh_ref, gl_ref, lh_ref, ll_ref, qd_ref, cov, wh, wl, linv, *packs):
    n = own_ref.shape[0]
    near = owner_ref.shape[1]
    nt = near + 1
    last = near * 128
    scale = math.sqrt(3.0) / length_scale

    def build(m, carry):
        pts = [
            [coords_ref[owner_ref[m, k], pl.ds(2 * slot_ref[m, k] + i, 1), :] * scale for i in range(2)]
            for k in range(near)
        ] + [[own_ref[m, i:i + 1] * scale for i in range(2)]]
        for i in range(nt):
            xc = jnp.broadcast_to(pts[i][0], (128, 128)).T
            yc = jnp.broadcast_to(pts[i][1], (128, 128)).T
            for j in range(i + 1):
                dx = xc - pts[j][0]
                dy = yc - pts[j][1]
                q = dx * dx + dy * dy
                s = q * lax.rsqrt(jnp.maximum(q, 1e-30))
                c = (1.0 + s) * jnp.exp(-s)
                if i == j:
                    diag = lax.broadcasted_iota(jnp.int32, (128, 128), 0) == lax.broadcasted_iota(
                        jnp.int32, (128, 128), 1
                    )
                    c = c + jnp.where(diag, nugget, 0.0)
                cov[m, i * 128:(i + 1) * 128, j * 128:(j + 1) * 128] = c
        return carry

    lax.fori_loop(0, n, build, 0)

    def terms(ref_h, ref_l, *at):
        return ref_h[at], ref_l[at]

    for j in range(nt):
        lo, hi = j * 128, (j + 1) * 128
        rows = slice(lo, hi)

        if j:
            def left(m, carry):
                a = (wh[m, lo:, :lo], wl[m, lo:, :lo])
                b = (wh[m, lo:hi, :lo], wl[m, lo:hi, :lo])
                cov[m, lo:, lo:hi] = cov[m, lo:, lo:hi] - wide(a, b, NT)
                return carry

            lax.fori_loop(0, n, left, 0)

        for m in range(n):
            packs[m // 2][:, (m % 2) * 64:(m % 2) * 64 + 64] = cov[m, lo:lo + 64, lo:lo + 64]
        eliminate(packs)
        for m in range(n):
            at = (m % 2) * 64
            top = split(lower64(packs[m // 2][:, at:at + 64]))
            w = split(small(split(cov[m, lo + 64:hi, lo:lo + 64]), top, NT))
            linv[j, m, 0:64, 0:64] = top[0].astype(jnp.float32) + top[1].astype(jnp.float32)
            linv[j, m, 0:64, 64:128] = jnp.zeros((64, 64), jnp.float32)
            linv[j, m, 64:128, 0:64] = small(w, top)
            linv[j, m, 64:128, 64:128] = cov[m, lo + 64:hi, lo + 64:hi] - small(w, w, NT)
        for m in range(n):
            packs[m // 2][:, (m % 2) * 64:(m % 2) * 64 + 64] = linv[j, m, 64:128, 64:128]
        eliminate(packs)
        for m in range(n):
            at = (m % 2) * 64
            low = lower64(packs[m // 2][:, at:at + 64])
            linv[j, m, 64:128, 64:128] = low
            linv[j, m, 64:128, 0:64] = -small(split(low), split(linv[j, m, 64:128, 0:64]))

        if j < near:
            def panel(m, carry):
                w = split(wide(split(cov[m, hi:, lo:hi]), split(linv[j, m]), NT))
                wh[m, hi:, lo:hi] = w[0]
                wl[m, hi:, lo:hi] = w[1]
                return carry

            lax.fori_loop(0, n, panel, 0)

    def back(m, carry):
        for k in reversed(range(near)):
            lo, hi = k * 128, (k + 1) * 128
            g = wh[m, last:, lo:hi].astype(jnp.float32) + wl[m, last:, lo:hi].astype(jnp.float32)
            if hi < last:
                g = g - wide((gh_ref[m, :, hi:last], gl_ref[m, :, hi:last]), (wh[m, hi:last, lo:hi], wl[m, hi:last, lo:hi]))
            gh_ref[m, :, lo:hi], gl_ref[m, :, lo:hi] = split(wide(split(g), split(linv[k, m])))
        li = linv[near, m]
        lh_ref[m], ll_ref[m] = split(li)
        qd_ref[m] = jnp.sum(li * li, axis=0, keepdims=True)
        return carry

    lax.fori_loop(0, n, back, 0)


def factor(owner, slot, coords_all, coords_own):
    n, near = owner.shape
    width = (near + 1) * 128
    return pl.pallas_call(
        factor_kernel,
        out_shape=(jax.ShapeDtypeStruct((n, 128, near * 128), jnp.bfloat16),) * 2
        + (jax.ShapeDtypeStruct((n, 128, 128), jnp.bfloat16),) * 2
        + (jax.ShapeDtypeStruct((n, 1, 128), jnp.float32),),
        in_specs=[pl.BlockSpec(memory_space=pltpu.SMEM)] * 2 + [pl.BlockSpec(memory_space=pltpu.VMEM)] * 2,
        out_specs=(pl.BlockSpec(memory_space=pltpu.VMEM),) * 5,
        scratch_shapes=[
            pltpu.VMEM((n, width, width), jnp.float32),
            pltpu.VMEM((n, width, width - 128), jnp.bfloat16),
            pltpu.VMEM((n, width, width - 128), jnp.bfloat16),
            pltpu.VMEM((near + 1, n, 128, 128), jnp.float32),
        ]
        + [pltpu.VMEM((64, 128), jnp.float32)] * (n // 2),
        compiler_params=pltpu.CompilerParams(vmem_limit_bytes=56 * 1024 * 1024),
        cost_estimate=pl.CostEstimate(flops=2_000_000_000, bytes_accessed=5_000_000, transcendentals=4_000_000),
        name="factor",
    )(owner, slot, coords_all, coords_own)


MESH = pl.DeviceIdType.MESH
SIDE = 4
ROUTES = (("x", "z", "y"), ("y", "x", "z"), ("z", "y", "x"))
CAP = 12


def coordinates(index):
    return {
        "z": index // (4 * SIDE * 2),
        "x": lax.rem(index // (2 * SIDE), SIDE),
        "c": lax.rem(index // SIDE, 2),
        "y": lax.rem(index, SIDE),
    }


def place():
    return coordinates(lax.axis_index("blk") * SIDE + lax.axis_index("nb"))


def device(at, **moved):
    to = {**at, **moved}
    return (to["z"] * (2 * SIDE) + to["x"] * 2 + to["c"], to["y"])


def ahead(at, axis, k):
    return lax.rem(at[axis] + (k + SIDE), SIDE)


def meet(partners):
    barrier = pltpu.get_barrier_semaphore()
    for partner in partners:
        pl.semaphore_signal(barrier, inc=1, device_id=partner, device_id_type=MESH)
    pl.semaphore_wait(barrier, len(partners))


class Sender:
    def __init__(self, at, send, recv):
        self.at, self.send, self.recv, self.made = at, send, recv, []

    def push(self, src, dst, **moved):
        n = len(self.made)
        copy = pltpu.make_async_remote_copy(
            src_ref=src, dst_ref=dst, send_sem=self.send.at[n], recv_sem=self.recv.at[n],
            device_id=device(self.at, **moved), device_id_type=MESH,
        )
        self.made.append(copy)
        return copy

    def start(self, src, dst, **moved):
        copy = self.push(src, dst, **moved)
        copy.start()
        return copy

    def finish(self):
        for copy in self.made:
            copy.wait_send()


def everywhere_kernel(x_ref, out_ref, own_sem, send, recv):
    at = place()
    sender = Sender(at, send, recv)
    own = pltpu.make_async_copy(x_ref, out_ref.at[at["z"], at["x"], at["c"], at["y"]], own_sem)
    own.start()
    meet([device(at, **{axis: ahead(at, axis, k)}) for axis in "yxz" for k in (1, 2, 3)] + [device(at, c=1 - at["c"])])
    line = out_ref.at[at["z"], at["x"], at["c"], at["y"]]
    stages = [
        [sender.push(x_ref, line, y=ahead(at, "y", k)) for k in (1, 2, 3)],
        [sender.push(out_ref.at[at["z"], at["x"], at["c"]], out_ref.at[at["z"], at["x"], at["c"]], x=ahead(at, "x", k)) for k in (1, 2, 3)],
        [sender.push(out_ref.at[at["z"], :, at["c"]], out_ref.at[at["z"], :, at["c"]], z=ahead(at, "z", k)) for k in (1, 2, 3)],
        [sender.push(out_ref.at[:, :, at["c"]], out_ref.at[:, :, at["c"]], c=1 - at["c"])],
    ]
    for number, stage in enumerate(stages):
        if number == 1:
            own.wait()
        for copy in stage:
            copy.start()
        for copy in stage:
            copy.wait_recv()
    sender.finish()


def everywhere(x, collective_id):
    out = pl.pallas_call(
        everywhere_kernel,
        out_shape=jax.ShapeDtypeStruct((SIDE, SIDE, 2, SIDE) + x.shape, x.dtype),
        in_specs=[pl.BlockSpec(memory_space=pltpu.VMEM)],
        out_specs=pl.BlockSpec(memory_space=pltpu.VMEM),
        scratch_shapes=[
            pltpu.SemaphoreType.DMA(()),
            pltpu.SemaphoreType.DMA((10,)),
            pltpu.SemaphoreType.DMA((10,)),
        ],
        compiler_params=pltpu.CompilerParams(collective_id=collective_id, has_side_effects=True),
        name="everywhere",
    )(x)
    return out.reshape((2 * SIDE ** 3,) + x.shape)


def deal_kernel(*refs):
    count = len(ROUTES)
    data, got, relay = refs[:count], refs[count:2 * count], refs[2 * count:3 * count]
    own_sem, send, recv = refs[3 * count:]
    at = place()
    c = at["c"]
    half = CAP // 2
    sender = Sender(at, send, recv)
    local = []
    for r, (axis, _, _) in enumerate(ROUTES):
        here = (at[axis], c)
        local.append(pltpu.make_async_copy(data[r].at[here], got[r].at[here], own_sem.at[r]))
        local[-1].start()
    meet(
        [device(at, **{axis: ahead(at, axis, k), "c": cc}) for axis in "xyz" for k in (1, -1) for cc in (0, 1)]
        + [device(at, c=1 - c)]
    )
    relays, plain = [], []
    for r, (axis, _, _) in enumerate(ROUTES):
        far = ahead(at, axis, 2)
        relays.append([
            sender.start(
                data[r].at[far, :, pl.ds(i * half, half)], relay[r].at[i], **{axis: ahead(at, axis, k)}
            )
            for i, k in enumerate((1, -1))
        ])
    for r, (axis, _, _) in enumerate(ROUTES):
        for k in (1, -1):
            to = ahead(at, axis, k)
            for cc in (c, 1 - c):
                plain.append(sender.start(data[r].at[to, cc], got[r].at[at[axis], c], **{axis: to, "c": cc}))
        plain.append(sender.start(data[r].at[at[axis], 1 - c], got[r].at[at[axis], c], c=1 - c))
    for r, (axis, _, _) in enumerate(ROUTES):
        for i, k in enumerate((1, -1)):
            relays[r][i].wait_recv()
            origin = ahead(at, axis, -k)
            for cc in (c, 1 - c):
                plain.append(sender.start(
                    relay[r].at[i, cc], got[r].at[origin, c, pl.ds(i * half, half)],
                    **{axis: ahead(at, axis, k), "c": cc},
                ))
    for copy in plain:
        copy.wait_recv()
    sender.finish()
    for copy in local:
        copy.wait()


def deal(data, collective_id):
    count = len(ROUTES)
    shapes = [jax.ShapeDtypeStruct(a.shape, a.dtype) for a in data]
    copies = (2 + 5 + 4) * count
    rows = data[0].shape[-2]
    return pl.pallas_call(
        deal_kernel,
        out_shape=tuple(shapes),
        in_specs=[pl.BlockSpec(memory_space=pl.ANY)] * count,
        out_specs=(pl.BlockSpec(memory_space=pl.ANY),) * count,
        scratch_shapes=[pltpu.VMEM((2, 2, CAP // 2, rows, 128), jnp.float32)] * count
        + [
            pltpu.SemaphoreType.DMA((count,)),
            pltpu.SemaphoreType.DMA((copies,)),
            pltpu.SemaphoreType.DMA((copies,)),
        ],
        compiler_params=pltpu.CompilerParams(collective_id=collective_id, has_side_effects=True),
        name="deal",
    )(*data)


def pile_kernel(*refs):
    count = len(ROUTES)
    meta, got, dense = refs[0], refs[1:1 + count], refs[1 + count:]
    g = pl.program_id(0)

    @pl.when(g == 0)
    def _():
        for d in dense:
            def clear(i, carry, d=d):
                d[pl.ds(8 * i, 8)] = jnp.zeros((8,) + d.shape[1:], jnp.float32)
                return carry

            lax.fori_loop(0, d.shape[0] // 8, clear, 0)

    for r in range(count):
        def add(i, carry, r=r):
            to = meta[(r * 2 * SIDE + g) * 128 + i]
            dense[r][to] = dense[r][to] + got[r][0, i]
            return carry

        lax.fori_loop(0, meta[(r * 2 * SIDE + g) * 128 + CAP], add, 0)


def pile(meta, got, places):
    count = len(ROUTES)
    rows = got[0].shape[-2]
    slab = pl.BlockSpec((1, CAP, rows, 128), lambda g, *m: (g, 0, 0, 0))
    whole = pl.BlockSpec((places, rows, 128), lambda g, *m: (0, 0, 0))
    return pl.pallas_call(
        pile_kernel,
        out_shape=(jax.ShapeDtypeStruct((places, rows, 128), jnp.float32),) * count,
        grid_spec=pltpu.PrefetchScalarGridSpec(
            num_scalar_prefetch=1,
            grid=(2 * SIDE,),
            in_specs=[slab] * count,
            out_specs=(whole,) * count,
        ),
        compiler_params=pltpu.CompilerParams(vmem_limit_bytes=54 * 1024 * 1024),
        name="pile",
    )(meta, *[a.reshape(2 * SIDE, CAP, rows, 128) for a in got])


def fold_kernel(scale, *refs):
    count = len(ROUTES)
    dense, (pull_ref, own_ref, weight_ref, latent_ref, new_ref, rms_ref) = refs[:count], refs[count:count + 6]
    refs = refs[count + 6:]
    mine, passing, direct, second = (refs[i * count:(i + 1) * count] for i in range(4))
    delta, line, total, own_sem, line_sem, send, recv = refs[4 * count:]
    at = place()
    sender = Sender(at, send, recv)
    ways = (1, -1)
    cut = (pl.ds(0, 2), pl.ds(2, 2))
    local = []
    for r, (_, f, _) in enumerate(ROUTES):
        local.append([pltpu.make_async_copy(dense[r].at[at[f]], mine[r].at[0], own_sem.at[r, 0])] + [
            pltpu.make_async_copy(dense[r].at[ahead(at, f, k), cut[i]], mine[r].at[1, cut[i]], own_sem.at[r, 1 + i])
            for i, k in enumerate(ways)
        ])
        for copy in local[r]:
            copy.start()
    meet(
        [device(at, **{axis: ahead(at, axis, k)}) for axis in "xyz" for k in (1, 2, 3)] + [device(at, c=1 - at["c"])]
    )
    ones, straight, twos, threes = [], [], [], []
    for r, (_, f, _) in enumerate(ROUTES):
        ones.append([
            sender.start(dense[r].at[ahead(at, f, 2), cut[i]], passing[r].at[0, cut[i]], **{f: ahead(at, f, k)})
            for i, k in enumerate(ways)
        ])
    for r, (_, f, _) in enumerate(ROUTES):
        straight.append([
            sender.start(dense[r].at[ahead(at, f, k), cut[1 - i]], direct[r].at[cut[1 - i]], **{f: ahead(at, f, k)})
            for i, k in enumerate(ways)
        ])
    for r, (_, f, _) in enumerate(ROUTES):
        twos.append([])
        for i, k in enumerate(ways):
            ones[r][i].wait_recv()
            local[r][1 + i].wait()
            mine[r][1, cut[i]] = mine[r][1, cut[i]] + passing[r][0, cut[i]]
            twos[r].append(sender.start(mine[r].at[1, cut[i]], passing[r].at[1, cut[i]], **{f: ahead(at, f, k)}))
    rows = new_ref.shape[-2] // count
    for r, (_, f, s) in enumerate(ROUTES):
        local[r][0].wait()
        for copy in straight[r] + twos[r]:
            copy.wait_recv()
        mine[r][0] = (mine[r][0] + direct[r][...]) + passing[r][1]
        threes.append([
            sender.start(mine[r].at[0, ahead(at, s, k)], second[r].at[k - 1], **{s: ahead(at, s, k)}) for k in (1, 2, 3)
        ])
    squares = []
    for r, (_, f, s) in enumerate(ROUTES):
        part = slice(r * rows, (r + 1) * rows)
        known = pull_ref[:, part, :] - own_ref[:, part, :]
        for copy in threes[r]:
            copy.wait_recv()
        prior = (mine[r][0, at[s]] + second[r][0]) + (second[r][1] + second[r][2])
        d = (known - prior) / weight_ref[:, part, :]
        delta[:, part, :] = d
        squares.append(jnp.sum(d * d, axis=0))
    squares.append(jnp.zeros((128 - rows * count, 128), jnp.float32))
    line[...] = jnp.sum(jnp.concatenate(squares, axis=0).T, axis=0, keepdims=True)
    here = total.at[at["z"], at["x"], at["c"], at["y"]]
    keep = pltpu.make_async_copy(line, here, line_sem)
    keep.start()
    keep.wait()
    plane, sheet, side = total.at[at["z"], at["x"], at["c"]], total.at[at["z"], :, at["c"]], total.at[:, :, at["c"]]
    for axis, src in (("y", here), ("x", plane), ("z", sheet)):
        stage = [sender.start(src, src, **{axis: ahead(at, axis, k)}) for k in (1, 2, 3)]
        for copy in stage:
            copy.wait_recv()
    sender.start(side, side, c=1 - at["c"]).wait_recv()
    spread = jnp.sum(total[...], axis=(0, 1, 2, 3))
    rms = jnp.sqrt(spread * scale + 1e-06)
    rms_ref[...] = rms
    step = jnp.broadcast_to(0.5 / rms, (128, 128)).T[:rows * count]
    for b in range(new_ref.shape[0]):
        new_ref[b] = latent_ref[b] + delta[b] * step
    sender.finish()


def fold(dense, pull, own_part, weight, latent, points, collective_id):
    count = len(ROUTES)
    slots = latent.shape[0]
    rows = dense[0].shape[-2]
    dense = [d.reshape(SIDE, SIDE, slots, rows, 128) for d in dense]
    part = (SIDE, slots, rows, 128)
    copies = (2 + 2 + 2 + 3) * count + 10
    return pl.pallas_call(
        functools.partial(fold_kernel, 1.0 / points),
        out_shape=(
            jax.ShapeDtypeStruct(latent.shape, jnp.float32),
            jax.ShapeDtypeStruct((1, 128), jnp.float32),
        ),
        in_specs=[pl.BlockSpec(memory_space=pl.ANY)] * count + [pl.BlockSpec(memory_space=pltpu.VMEM)] * 4,
        out_specs=(pl.BlockSpec(memory_space=pltpu.VMEM),) * 2,
        scratch_shapes=[pltpu.VMEM((2,) + part, jnp.float32)] * count
        + [pltpu.VMEM((2,) + part, jnp.float32)] * count
        + [pltpu.VMEM(part, jnp.float32)] * count
        + [pltpu.VMEM((SIDE - 1,) + part[1:], jnp.float32)] * count
        + [
            pltpu.VMEM(latent.shape, jnp.float32),
            pltpu.VMEM((1, 128), jnp.float32),
            pltpu.VMEM((SIDE, SIDE, 2, SIDE, 1, 128), jnp.float32),
            pltpu.SemaphoreType.DMA((count, 3)),
            pltpu.SemaphoreType.DMA(()),
            pltpu.SemaphoreType.DMA((copies,)),
            pltpu.SemaphoreType.DMA((copies,)),
        ],
        compiler_params=pltpu.CompilerParams(
            collective_id=collective_id, has_side_effects=True, vmem_limit_bytes=40 * 1024 * 1024
        ),
        name="fold",
    )(*dense, pull, own_part, weight, latent)


def apply_kernel(routes, near, *refs):
    pos = refs[1]
    v, refs = refs[2:2 + near], refs[2 + near:]
    own_ref, gh_ref, gl_ref, lh_ref, ll_ref = refs[:5]
    outs, u_ref = refs[5:5 + routes], refs[5 + routes]
    keep, sem = refs[6 + routes:]
    b = pl.program_id(0)
    n = pl.num_programs(0)
    slot = lax.rem(b, 2)
    rows = outs[0].shape[1]

    def copies(b, slot):
        return [
            pltpu.make_async_copy(
                keep.at[slot, k, pl.ds(r * rows, rows)],
                outs[r].at[pos[(r * n + b) * near + k]],
                sem.at[slot, k, r],
            )
            for k in range(near)
            for r in range(routes)
        ]

    values = jnp.concatenate([v[k][0] for k in range(near)], axis=1)
    low = (lh_ref[0], ll_ref[0])
    g = (gh_ref[0], gl_ref[0])
    rest = own_ref[0] - wide(split(values), g, NT)
    u = wide(split(wide(split(rest), low, NT)), low)
    u_ref[0] = u
    pulled = -wide(split(u), g)

    @pl.when(b >= 2)
    def _():
        for copy in copies(b - 2, slot):
            copy.wait()

    for k in range(near):
        keep[slot, k] = pulled[:, k * 128:(k + 1) * 128]
    for copy in copies(b, slot):
        copy.start()

    @pl.when(b == n - 1)
    def _():
        for copy in copies(b - 1, 1 - slot):
            copy.wait()
        for copy in copies(b, slot):
            copy.wait()


def apply_blocks(nbr, positions, length, latent_all, latent, gh, gl, lh, ll):
    n, fields, points = latent.shape
    routes = len(ROUTES)
    near = nbr.shape[1]
    rows = fields // routes

    def v_spec(k):
        return pl.BlockSpec((1, fields, points), lambda b, nbr, pos: (nbr[b * near + k], 0, 0))

    def b_spec(*shape):
        return pl.BlockSpec((1,) + shape, lambda b, nbr, pos: (b, 0, 0))

    return pl.pallas_call(
        functools.partial(apply_kernel, routes, near),
        out_shape=(jax.ShapeDtypeStruct((length, rows, points), jnp.float32),) * routes
        + (jax.ShapeDtypeStruct(latent.shape, jnp.float32),),
        grid_spec=pltpu.PrefetchScalarGridSpec(
            num_scalar_prefetch=2,
            grid=(n,),
            in_specs=[v_spec(k) for k in range(near)]
            + [b_spec(fields, points)]
            + [b_spec(points, near * points)] * 2
            + [b_spec(points, points)] * 2,
            out_specs=(pl.BlockSpec(memory_space=pl.ANY),) * routes + (b_spec(fields, points),),
            scratch_shapes=[
                pltpu.VMEM((2, near, fields, points), jnp.float32),
                pltpu.SemaphoreType.DMA((2, near, routes)),
            ],
        ),
        name="apply",
    )(nbr.reshape(-1), positions, *([latent_all] * near), latent, gh, gl, lh, ll)


def probit_ratio(margin):
    density = jnp.exp(-0.5 * margin * margin - 0.5 * math.log(2.0 * math.pi))
    mass = 0.5 * lax.erfc(-margin / math.sqrt(2.0))
    return density / mass


def rank_of(keys):
    count = keys.shape[-1]
    earlier = lax.broadcasted_iota(jnp.int32, (count, count), 1) < lax.broadcasted_iota(
        jnp.int32, (count, count), 0
    )
    same = keys[..., None, :] == keys[..., :, None]
    return jnp.sum(jnp.where(same & earlier, 1, 0), axis=-1).astype(jnp.int32)


def tables(at, named, places, slots):
    out = []
    for sparse, one, two in ROUTES:
        group_of = []
        for a in range(SIDE):
            for c in range(2):
                blk, nb = device({**at, sparse: a, "c": c})
                group_of.append(blk * SIDE + nb)
        rows = jnp.stack(group_of)
        asked, slot = named[rows], places[rows]
        lies = coordinates(asked)
        mine = (lies[sparse] == at[sparse]) & (lies["c"] == at["c"])
        to = (lies[one] * SIDE + lies[two]) * slots + slot
        keys = jnp.where(mine, 1, 0)
        rank = jnp.where(mine, rank_of(keys), -1)
        lane = lax.broadcasted_iota(jnp.int32, (2 * SIDE, 128, 1), 1)
        meta = jnp.sum(jnp.where(rank[:, None, :] == lane, to[:, None, :], 0), axis=2)
        meta = jnp.where(lane[:, :, 0] == CAP, jnp.sum(keys, axis=1)[:, None], meta)
        out.append(meta.astype(jnp.int32).reshape(-1))
    return jnp.concatenate(out)


def body(latent, coords, labels, owner, slot):
    block_count, field_count, point_count = latent.shape
    near_count = owner.shape[1]
    items = block_count * near_count
    axes = ("blk", "nb")
    device_count = lax.axis_size("blk") * lax.axis_size("nb")
    routes = len(ROUTES)
    rows = field_count // routes
    length = 2 * SIDE * CAP
    at = place()
    wanted = owner.reshape(-1)
    places = slot.reshape(-1)
    lies = coordinates(wanted)
    positions, most = [], 0
    for sparse, _, _ in ROUTES:
        group = lies[sparse] * 2 + lies["c"]
        rank = rank_of(group)
        most = jnp.maximum(most, jnp.max(rank))
        positions.append(group * CAP + jnp.minimum(rank, CAP - 1))
    flag = jnp.where(most >= CAP, 1, 0)
    line = jnp.concatenate([wanted, places, flag[None], jnp.zeros((127 - 2 * items,), jnp.int32)])
    note = jnp.concatenate(
        [
            coords.reshape(2 * block_count, point_count),
            jnp.broadcast_to(line.astype(jnp.float32)[None], (8, point_count)),
        ]
    )
    notes = everywhere(note, 1)
    latent_all = lax.all_gather(latent, axes, axis=0, tiled=True)
    lines = notes[:, 2 * block_count, :].astype(jnp.int32)
    crowded = jnp.max(lines[:, 2 * items]) > 0
    meta = tables(at, lines[:, :items], lines[:, items:2 * items], block_count)
    order = lax.broadcasted_iota(jnp.int32, (items,), 0)
    positions = jnp.concatenate([jnp.where(crowded, order, p) for p in positions])
    capacity = max(2, 2 * items // device_count)

    def requests():
        position = wanted * capacity + rank_of(wanted)
        sent = jnp.full((device_count * capacity,), -1, jnp.int32).at[position].set(places)
        asked = lax.all_to_all(
            sent.reshape(device_count, capacity), axes, split_axis=0, concat_axis=0, tiled=True
        ).reshape(-1)
        return position, asked

    def exchange(x):
        return lax.all_to_all(
            x.reshape(device_count, capacity, field_count, point_count),
            axes, split_axis=0, concat_axis=0, tiled=True,
        ).reshape(device_count * capacity, field_count, point_count)

    gh, gl, lh, ll, qdiag = factor(owner, slot, notes, coords)
    *data, own_part = apply_blocks(
        owner * block_count + slot, positions, length, latent_all, latent, gh, gl, lh, ll
    )

    sign = 2.0 * labels.astype(jnp.float32) - 1.0
    margin = sign * latent
    ratio = probit_ratio(margin)
    pull = sign * ratio
    weight = ratio * (ratio + margin) + qdiag
    point_total = block_count * point_count * device_count

    def routed_return():
        back = deal([d.reshape(SIDE, 2, CAP, rows, point_count) for d in data], 5)
        sums = pile(meta, back, SIDE * SIDE * block_count)
        new_latent, rms = fold(sums, pull, own_part, weight, latent, point_total, 4)
        return new_latent, rms[0, :field_count]

    def padded_return():
        position, asked = requests()
        near = jnp.concatenate([d[:items] for d in data], axis=1)
        outgoing = jnp.zeros((device_count * capacity, field_count, point_count), jnp.float32)
        returned = exchange(outgoing.at[position].set(near))
        returned = jnp.where((asked >= 0)[:, None, None], returned, 0.0)
        prior = own_part.at[jnp.maximum(asked, 0)].add(returned)
        delta = (pull - prior) / weight
        partial = jnp.sum(delta * delta, axis=(0, 2))
        spread = jnp.sum(everywhere(jnp.pad(partial, (0, 128 - field_count))[None], 2), axis=(0, 1))[:field_count]
        step_rms = jnp.sqrt(spread / point_total + 1e-06)
        return latent + 0.5 * delta / step_rms[None, :, None], step_rms

    return lax.cond(crowded, padded_return, routed_return)


def solution(mesh):
    both = ("blk", "nb")
    return jax.shard_map(
        body,
        mesh=mesh,
        in_specs=(P(both, None, None), P(both, None, None), P(both, None, None), P(both, None), P(both, None)),
        out_specs=(P(both, None, None), P()),
        check_vma=False,
    )
```
